32 devices in a mesh: wide: 8 (over y, x, core), tensor: 4 (over z).
Axes of the slice: x: 2, y: 2, z: 4, core: 2. Of those that a mesh axis runs over, the one named last changes fastest.
Arguments:
- tokens: bfloat16 [8192, 2048], P(('wide', 'tensor')), may hold values from -6 to 6
- query_weight: bfloat16 [2048, 2048], P('wide', 'tensor'), may hold values from -0.125 to 0.125
- key_weight: bfloat16 [2048, 2048], P('wide', 'tensor'), may hold values from -0.125 to 0.125
- value_weight: bfloat16 [2048, 3456], P('wide', 'tensor'), may hold values from -0.125 to 0.125
- swish_weight: bfloat16 [2048, 3456], P('wide', 'tensor'), may hold values from -0.125 to 0.125
- output_weight: bfloat16 [3456, 2048], P('tensor', 'wide'), may hold values from -0.21875 to 0.21875
- mlp_gate: bfloat16 [2048, 3456], P('wide', 'tensor'), may hold values from -0.125 to 0.125
- mlp_up: bfloat16 [2048, 3456], P('wide', 'tensor'), may hold values from -0.125 to 0.125
- mlp_down: bfloat16 [3456, 2048], P('tensor', 'wide'), may hold values from -0.21875 to 0.21875
- gain_one: float32 [2048], replicated, may hold values from 0.5 to 1.5
- gain_two: float32 [2048], replicated, may hold values from 0.5 to 1.5
- segments: int32 [8, 1024], P('wide'), may hold values from 0 to 5, never falling along the last dimension, each value on 1 to 512 neighbouring positions
- decay_rate: float32 [8], P('tensor'), may hold values from 0.0005 to 0.05
- cotangent: bfloat16 [8192, 2048], P(('wide', 'tensor')), may hold values from -6 to 6
Outputs:
- layer_out: bfloat16 [8192, 2048], P(('wide', 'tensor'))
- input_grad: float32 [8192, 2048], P(('wide', 'tensor'))
- query_grad: float32 [2048, 2048], P('wide', 'tensor')
- key_grad: float32 [2048, 2048], P('wide', 'tensor')
- value_grad: float32 [2048, 3456], P('wide', 'tensor')
- swish_grad: float32 [2048, 3456], P('wide', 'tensor')
- output_grad: float32 [3456, 2048], P('tensor', 'wide')
- gate_grad: float32 [2048, 3456], P('wide', 'tensor')
- up_grad: float32 [2048, 3456], P('wide', 'tensor')
- down_grad: float32 [3456, 2048], P('tensor', 'wide')
- gain_one_grad: float32 [2048], replicated
- gain_two_grad: float32 [2048], replicated
The draws below stay inside these ranges and needn't reach their ends.
Inputs may be any that keep to these rules, and one draw needn't show every extreme that they name: `segments`: in each row the numbers never fall; a document holds 1 to 512 tokens and one holds exactly 512.
All inputs are finite; a program needn't handle non-finite values.
Results may differ from the reference program's by a relative error of at most 0.02.
The reference program's roundings to bfloat16 on the way count: a program that leaves them out, or rounds other values in their place, can miss the bound.
Values may be sent and summed in bfloat16 or wider, within the bound.
No kernel may reach another device: no remote copies, remote signals or barrier semaphores. Data moves between devices by JAX's collectives and lax.ppermute only.
A program may use at most 192 MiB of HBM per device.

```python
import math
import jax
import jax.numpy as jnp
import numpy as np
from jax import lax

D = 2048
HEADS = 8
KEY = 256
VAL = 432
FF = 3456
KD = 2048
VD = 3456
LEN = 1024
SEQS = 8
TOKENS = 8192


def block_scale(key, dims, split, smallest, largest):
    def one(dim, blocks):
        steps = jax.random.uniform(jax.random.fold_in(jax.random.fold_in(key, 6), dim), (blocks,), jnp.float32, smallest / len(split), largest / len(split))
        return jnp.repeat(jnp.exp(steps), dims[dim] // blocks).reshape((-1,) + (1,) * (len(dims) - dim - 1))

    level = one(*split[0])
    for cut in split[1:]:
        level = level * one(*cut)
    return level


def profile(amount, total, reach, lean):
    loads = [(1 << 20) // math.isqrt(grade ** lean) + 1 for grade in range(2, amount + 1)]
    spare, given = total - reach - (amount - 1), [1] * (amount - 1)
    while spare > 0:
        free = [i for i in range(amount - 1) if given[i] < reach]
        whole, remaining = sum([loads[i] for i in free]), spare
        for i in free:
            extra = min(reach - given[i], max(1, remaining * loads[i] // whole), spare)
            given[i] = given[i] + extra
            spare = spare - extra
    return np.array([reach] + given)


def uneven(stream_key, number_of, total, bound, skew):
    if number_of == 2:
        one = jax.random.randint(stream_key, (), max(1, total - bound), min(bound, total - 1) + 1)
        return jnp.stack([one, total - one])
    lengths = jnp.asarray(profile(number_of, total, bound, skew), jnp.int32)
    twos = (number_of - 1) // 2
    donor, taker = lengths[1:1 + 2 * twos:2], lengths[2:2 + 2 * twos:2]
    slack = jnp.minimum(donor - 1, bound - taker)
    shifted = jax.random.randint(jax.random.fold_in(stream_key, 1), (twos,), 0, 1 << 20) % (slack + 1)
    lengths = lengths.at[1:1 + 2 * twos:2].set(donor - shifted).at[2:2 + 2 * twos:2].set(taker + shifted)
    return lengths[jax.random.permutation(jax.random.fold_in(stream_key, 2), number_of)]


def noise(own_key, shape, deviation, bound, cuts=(), kind=jnp.bfloat16):
    drawn = deviation * jax.random.normal(own_key, shape, jnp.float32)
    if cuts:
        drawn = drawn * block_scale(own_key, shape, cuts, -0.22, 0.18)
    return jnp.clip(drawn, -bound, bound).astype(kind)


def setup_inputs(seed: int = 0) -> dict:
    key_list = jax.random.split(jax.random.key(seed), 15)
    tokens = noise(key_list[0], (TOKENS, D), 1.0, 6.0, ((0, 32),))
    query_weight = noise(key_list[1], (D, KD), D ** -0.5, 0.125, ((0, 8), (1, 4)))
    key_weight = noise(key_list[2], (D, KD), D ** -0.5, 0.125, ((0, 8), (1, 4)))
    value_weight = noise(key_list[3], (D, VD), D ** -0.5, 0.125, ((0, 8), (1, 4)))
    swish_weight = noise(key_list[4], (D, VD), D ** -0.5, 0.125, ((0, 8), (1, 4)))
    output_weight = noise(key_list[5], (VD, D), (VD // 4) ** -0.5, 0.21875, ((0, 4), (1, 8)))
    mlp_gate = noise(key_list[6], (D, FF), D ** -0.5, 0.125, ((0, 8), (1, 4)))
    mlp_up = noise(key_list[7], (D, FF), D ** -0.5, 0.125, ((0, 8), (1, 4)))
    mlp_down = noise(key_list[8], (FF, D), (FF // 4) ** -0.5, 0.21875, ((0, 4), (1, 8)))
    gain_one = jnp.clip(1.0 + 0.1 * jax.random.normal(key_list[9], (D,), jnp.float32), 0.5, 1.5)
    gain_two = jnp.clip(1.0 + 0.1 * jax.random.normal(key_list[10], (D,), jnp.float32), 0.5, 1.5)
    segments = jax.vmap(lambda own: jnp.searchsorted(jnp.cumsum(uneven(own, 6, LEN, LEN // 2, 2)), jnp.arange(LEN), side="right"))(jax.random.split(key_list[11], SEQS)).reshape((SEQS, LEN)).astype(jnp.int32)
    decay_rate = jnp.clip(jnp.exp(math.log(0.05) - 4.6051702 * jax.random.uniform(key_list[12], (HEADS,), jnp.float32) ** block_scale(key_list[12], (HEADS,), ((0, 4),), -0.2, 0.2)), 0.0005, 0.05)
    cotangent = noise(key_list[13], (TOKENS, D), 1.0, 6.0, ((0, 32),))
    return dict(tokens=tokens, query_weight=query_weight, key_weight=key_weight, value_weight=value_weight, swish_weight=swish_weight, output_weight=output_weight, mlp_gate=mlp_gate, mlp_up=mlp_up, mlp_down=mlp_down, gain_one=gain_one, gain_two=gain_two, segments=segments, decay_rate=decay_rate, cotangent=cotangent)


@jax.custom_vjp
def low(v):
    return lax.optimization_barrier(v.astype(jnp.bfloat16)).astype(jnp.float32)

@jax.custom_vjp
def low_back(v):
    return v

def low_keep(v):
    return (low(v), None)

def low_pass(kept, grad):
    return (grad,)

def back_keep(v):
    return (v, None)

def back_low(kept, grad):
    return (low(grad),)
low.defvjp(low_keep, low_pass)
low_back.defvjp(back_keep, back_low)

def rms_norm(rows, gain):
    scale = lax.rsqrt(lax.optimization_barrier(jnp.mean(rows * rows, axis=-1, keepdims=True)) + 1e-06)
    return rows * scale * gain

def matmul(left, right):
    return jnp.dot(left, right, precision=lax.Precision.HIGHEST, preferred_element_type=jnp.float32)

def retain_one(query, keys, values, segment, decay_rate):
    position = jnp.arange(LEN, dtype=jnp.int32)
    difference = position[:, None] - position[None, :]
    allowed = (difference >= 0) & (segment[:, None] == segment[None, :])
    gap = jnp.maximum(difference, 0).astype(decay_rate.dtype)
    weight = jnp.where(allowed[None], jnp.exp(-decay_rate[:, None, None] * gap[None]), 0.0)
    scores = low_back(jnp.einsum('nhk,mhk->hnm', query, keys, precision=lax.Precision.HIGHEST))
    probs = low(scores * weight)
    return low_back(jnp.einsum('hnm,mhv->nhv', probs, values, precision=lax.Precision.HIGHEST))

def forward(tokens, query_weight, key_weight, value_weight, swish_weight, output_weight, mlp_gate, mlp_up, mlp_down, gain_one, gain_two, segments, decay_rate):
    normed = low(rms_norm(tokens, gain_one))
    query = low(low_back(matmul(normed, query_weight)))
    keys = low(low_back(matmul(normed, key_weight)))
    values = low(low_back(matmul(normed, value_weight)))
    gate_pre = low_back(matmul(normed, swish_weight))
    step_fn = jax.checkpoint(retain_one)

    def one_sequence(carry, item):
        q_seq, k_seq, v_seq, seg_seq = item
        return (carry, step_fn(q_seq, k_seq, v_seq, seg_seq, decay_rate))
    unused, mixed = lax.scan(one_sequence, jnp.zeros((), jnp.float32), (query.reshape(SEQS, LEN, HEADS, KEY), keys.reshape(SEQS, LEN, HEADS, KEY), values.reshape(SEQS, LEN, HEADS, VAL), segments))
    mixed = mixed.reshape(TOKENS, HEADS, VAL)
    centred = mixed - lax.optimization_barrier(jnp.mean(mixed, axis=-1, keepdims=True))
    grouped = centred * lax.rsqrt(lax.optimization_barrier(jnp.mean(centred * centred, axis=-1, keepdims=True)) + 1.0)
    gated = low(jax.nn.silu(gate_pre) * grouped.reshape(TOKENS, VD))
    middle = tokens + low_back(matmul(gated, output_weight))
    normed_two = low(rms_norm(middle, gain_two))
    gate_mlp = low_back(matmul(normed_two, mlp_gate))
    up_mlp = low_back(matmul(normed_two, mlp_up))
    hidden = low(jax.nn.gelu(gate_mlp, approximate=True) * up_mlp)
    return middle + low_back(matmul(hidden, mlp_down))

def reference(tokens, query_weight, key_weight, value_weight, swish_weight, output_weight, mlp_gate, mlp_up, mlp_down, gain_one, gain_two, segments, decay_rate, cotangent):
    floats = (tokens.astype(jnp.float32), query_weight.astype(jnp.float32), key_weight.astype(jnp.float32), value_weight.astype(jnp.float32), swish_weight.astype(jnp.float32), output_weight.astype(jnp.float32), mlp_gate.astype(jnp.float32), mlp_up.astype(jnp.float32), mlp_down.astype(jnp.float32), gain_one.astype(jnp.float32), gain_two.astype(jnp.float32))
    rates = decay_rate.astype(jnp.float32)
    segment_ids = segments.astype(jnp.int32)

    def wrapped(*arrays):
        return forward(*arrays, segment_ids, rates)
    result, pullback = jax.vjp(wrapped, *floats)
    grads = pullback(cotangent.astype(jnp.float32))
    return (result.astype(jnp.bfloat16), grads[0], grads[1], grads[2], grads[3], grads[4], grads[5], grads[6], grads[7], grads[8], grads[9], grads[10])
```

```python
from functools import partial

import jax
import jax.numpy as jnp
from jax import lax
from jax.experimental import pallas as pl
from jax.experimental.pallas import tpu as pltpu
from jax.sharding import PartitionSpec as P

KEY = 256
VAL = 432
PAD = 512
BF = jnp.bfloat16
F32 = jnp.float32
VMEM_LIMIT = 48 * 1024 * 1024


def round_up(count, step):
    return -(-count // step) * step


def permute_kernel(index, source, target):
    target[...] = source[...]


def permute_blocks(array, index):
    rows, features = array.shape
    count = index.shape[0]
    width = features // count
    return pl.pallas_call(
        permute_kernel,
        grid_spec=pltpu.PrefetchScalarGridSpec(
            num_scalar_prefetch=1,
            grid=(count,),
            in_specs=[pl.BlockSpec((rows, width), lambda j, index: (0, index[j]))],
            out_specs=pl.BlockSpec((rows, width), lambda j, index: (0, j)),
        ),
        out_shape=jax.ShapeDtypeStruct(array.shape, array.dtype),
        cost_estimate=pl.CostEstimate(
            flops=0, transcendentals=0, bytes_accessed=2 * array.size * array.dtype.itemsize
        ),
        name="permute_blocks",
    )(index, array)


def weight_block(rate, row_seg, col_seg, offset, block):
    down = lax.broadcasted_iota(jnp.int32, (block, block), 0)
    across = lax.broadcasted_iota(jnp.int32, (block, block), 1)
    gap = offset + down - across
    allowed = (gap >= 0) & (row_seg == col_seg)
    return jnp.where(allowed, jnp.exp(-rate * jnp.maximum(gap, 0).astype(F32)), 0.0)


def normalize(mixed):
    lane = lax.broadcasted_iota(jnp.int32, mixed.shape, 1)
    valid = lane < VAL
    mean = jnp.sum(mixed, axis=-1, keepdims=True) * (1.0 / VAL)
    centred = jnp.where(valid, mixed - mean, 0.0)
    inverse = lax.rsqrt(jnp.sum(centred * centred, axis=-1, keepdims=True) * (1.0 / VAL) + 1.0)
    return centred * inverse, inverse, valid


def dot_nt(left, right):
    return lax.dot_general(left, right, (((1,), (1,)), ((), ())), preferred_element_type=F32)


def dot_tn(left, right):
    return lax.dot_general(left, right, (((0,), (0,)), ((), ())), preferred_element_type=F32)


def dot_nn(left, right):
    return lax.dot_general(left, right, (((1,), (0,)), ((), ())), preferred_element_type=F32)


def forward_kernel(block, steps, rate, seg_col, seg_row, q, k, v, z, gated, mixed, acc):
    head, at = pl.program_id(0), pl.program_id(1)
    decay = rate[head]
    acc[...] = jnp.zeros_like(acc)
    for step in range(steps):

        @pl.when(step <= at)
        def _():
            cols = pl.ds(step * block, block)
            weight = weight_block(decay, seg_col[...], seg_row[:, cols], (at - step) * block, block)
            probs = (dot_nt(q[...], k[cols, :]) * weight).astype(BF)
            acc[...] += dot_nn(probs, v[cols, :])

    total = acc[...]
    grouped, _, _ = normalize(total)
    mixed[...] = total
    gate = z[...]
    gated[...] = (gate * jax.nn.sigmoid(gate) * grouped).astype(BF)


def retain_forward(qkv, gate_pre, seg_row, seg_col, rate):
    total = qkv.shape[0]
    heads = rate.shape[0]
    block = min(256, total)
    steps = total // block
    pairs = steps * (steps + 1) // 2 * heads
    return pl.pallas_call(
        partial(forward_kernel, block, steps),
        grid=(heads, steps),
        in_specs=[
            pl.BlockSpec(memory_space=pltpu.SMEM),
            pl.BlockSpec((block, 1), lambda h, i: (i, 0)),
            pl.BlockSpec((1, total), lambda h, i: (0, 0)),
            pl.BlockSpec((block, KEY), lambda h, i: (i, h)),
            pl.BlockSpec((total, KEY), lambda h, i: (0, heads + h)),
            pl.BlockSpec((total, PAD), lambda h, i: (0, heads + h)),
            pl.BlockSpec((block, PAD), lambda h, i: (i, h)),
        ],
        out_specs=[
            pl.BlockSpec((block, PAD), lambda h, i: (i, h)),
            pl.BlockSpec((block, PAD), lambda h, i: (i, h)),
        ],
        out_shape=[
            jax.ShapeDtypeStruct((total, heads * PAD), BF),
            jax.ShapeDtypeStruct((total, heads * PAD), F32),
        ],
        scratch_shapes=[pltpu.VMEM((block, PAD), F32)],
        compiler_params=pltpu.CompilerParams(vmem_limit_bytes=VMEM_LIMIT),
        cost_estimate=pl.CostEstimate(
            flops=2 * pairs * block * block * (KEY + PAD),
            transcendentals=pairs * block * block,
            bytes_accessed=total * heads * (KEY * 4 + PAD * 12),
        ),
        name="retain_forward",
    )(rate, seg_col, seg_row, qkv, qkv, qkv, gate_pre)


def backward_kernel(
    block, steps, rate, seg_col, seg_row, q, k, v, z, mixed, dy, dq, dk, dv, dz, dk_acc, dv_acc, dq_acc
):
    head, at = pl.program_id(0), pl.program_id(1)
    decay = rate[head]

    @pl.when(at == 0)
    def _():
        dk_acc[...] = jnp.zeros_like(dk_acc)
        dv_acc[...] = jnp.zeros_like(dv_acc)

    grouped, inverse, valid = normalize(mixed[...])
    gate, upstream = z[...], dy[...]
    sig = jax.nn.sigmoid(gate)
    dz[...] = (upstream * grouped * (sig + gate * sig * (1.0 - sig))).astype(BF)
    dg = upstream * (gate * sig)
    first = jnp.sum(dg, axis=-1, keepdims=True) * (1.0 / VAL)
    second = jnp.sum(dg * grouped, axis=-1, keepdims=True) * (1.0 / VAL)
    do = jnp.where(valid, inverse * (dg - first - grouped * second), 0.0).astype(BF)
    dq_acc[...] = jnp.zeros_like(dq_acc)
    for step in range(steps):

        @pl.when(step <= at)
        def _():
            cols = pl.ds(step * block, block)
            weight = weight_block(decay, seg_col[...], seg_row[:, cols], (at - step) * block, block)
            probs = (dot_nt(q[...], k[cols, :]) * weight).astype(BF)
            score_grad = (dot_nt(do, v[cols, :]) * weight).astype(BF)
            dq_acc[...] += dot_nn(score_grad, k[cols, :])
            dk_acc[cols, :] += dot_tn(score_grad, q[...])
            dv_acc[cols, :] += dot_tn(probs, do)

    dq[...] = dq_acc[...].astype(BF)

    @pl.when(at == steps - 1)
    def _():
        dk[...] = dk_acc[...].astype(BF)
        dv[...] = dv_acc[...].astype(BF)


def retain_backward(qkv, gate_pre, mixed, dy, seg_row, seg_col, rate):
    total = qkv.shape[0]
    heads = rate.shape[0]
    block = min(256, total)
    steps = total // block
    pairs = steps * (steps + 1) // 2 * heads
    return pl.pallas_call(
        partial(backward_kernel, block, steps),
        grid=(heads, steps),
        in_specs=[
            pl.BlockSpec(memory_space=pltpu.SMEM),
            pl.BlockSpec((block, 1), lambda h, i: (i, 0)),
            pl.BlockSpec((1, total), lambda h, i: (0, 0)),
            pl.BlockSpec((block, KEY), lambda h, i: (i, h)),
            pl.BlockSpec((total, KEY), lambda h, i: (0, heads + h)),
            pl.BlockSpec((total, PAD), lambda h, i: (0, heads + h)),
            pl.BlockSpec((block, PAD), lambda h, i: (i, h)),
            pl.BlockSpec((block, PAD), lambda h, i: (i, h)),
            pl.BlockSpec((block, PAD), lambda h, i: (i, h)),
        ],
        out_specs=[
            pl.BlockSpec((block, KEY), lambda h, i: (i, h)),
            pl.BlockSpec((total, KEY), lambda h, i: (0, h)),
            pl.BlockSpec((total, PAD), lambda h, i: (0, h)),
            pl.BlockSpec((block, PAD), lambda h, i: (i, h)),
        ],
        out_shape=[
            jax.ShapeDtypeStruct((total, heads * KEY), BF),
            jax.ShapeDtypeStruct((total, heads * KEY), BF),
            jax.ShapeDtypeStruct((total, heads * PAD), BF),
            jax.ShapeDtypeStruct((total, heads * PAD), BF),
        ],
        scratch_shapes=[
            pltpu.VMEM((total, KEY), F32),
            pltpu.VMEM((total, PAD), F32),
            pltpu.VMEM((block, KEY), F32),
        ],
        compiler_params=pltpu.CompilerParams(vmem_limit_bytes=VMEM_LIMIT),
        cost_estimate=pl.CostEstimate(
            flops=2 * pairs * block * block * (3 * KEY + 2 * PAD),
            transcendentals=pairs * block * block,
            bytes_accessed=total * heads * (KEY * 8 + PAD * 18),
        ),
        name="retain_backward",
    )(rate, seg_col, seg_row, qkv, qkv, qkv, gate_pre, mixed, dy)


def swap_wide(array, mask):
    count = lax.axis_size("wide")
    return lax.ppermute(array, "wide", [(i, i ^ mask) for i in range(count)])


def swap_tensor(array, mask):
    count = lax.axis_size("tensor")
    return lax.ppermute(array, "tensor", [(i, i ^ mask) for i in range(count)])


def swap_halves(array):
    half = array.shape[1] // 2
    return jnp.concatenate([array[:, half:], array[:, :half]], axis=1)


def top_bit():
    return lax.axis_size("wide").bit_length() - 2


def mask_of(bit):
    return 1 if bit == top_bit() else 2 << bit


def take(array, places, axis, width):
    runs = []
    for place in places:
        if runs and runs[-1][1] == place:
            runs[-1][1] = place + 1
        else:
            runs.append([place, place + 1])
    parts = [lax.slice_in_dim(array, a * width, b * width, axis=axis) for a, b in runs]
    return parts[0] if len(parts) == 1 else jnp.concatenate(parts, axis=axis)


def gather_pieces(start, bits):
    pieces = dict(start)
    for bit in bits:
        for number in list(pieces):
            pieces[number | 1 << bit] = swap_wide(pieces[number], mask_of(bit))
    return [pieces[number] for number in range(len(pieces))]


def reduce_blocks(array, axis, bits, exact_last):
    count = lax.axis_size("wide")
    width = array.shape[axis] // count
    numbers = list(range(count))
    for place, bit in enumerate(bits):
        away = [i for i, number in enumerate(numbers) if number >> bit & 1]
        kept = [i for i, number in enumerate(numbers) if not number >> bit & 1]
        received = swap_wide(take(array, away, axis, width), mask_of(bit))
        array = take(array, kept, axis, width).astype(F32) + received.astype(F32)
        if not (exact_last and place == len(bits) - 1):
            array = array.astype(BF)
        numbers = [numbers[i] for i in kept]
    return array


def unit_pairs(shift_even, shift_odd):
    wide, tensor = lax.axis_size("wide"), lax.axis_size("tensor")
    pairs = []
    for w in range(wide):
        for t in range(tensor):
            over_w, over_t = shift_odd if w & 1 else shift_even
            pairs.append((w * tensor + t, (w ^ over_w) * tensor + (t ^ over_t)))
    return pairs


def swap_both(array, shift_even, shift_odd):
    return lax.ppermute(array, ("wide", "tensor"), unit_pairs(shift_even, shift_odd))


def gather_units(block, axis, bits):
    first = swap_both(block, (0, 0), (0, 2))
    second = swap_both(block, (1, 2), (1, 0))
    mask = 4
    while mask < lax.axis_size("tensor"):
        first = jnp.concatenate([first, swap_tensor(first, mask)], axis=axis)
        second = jnp.concatenate([second, swap_tensor(second, mask)], axis=axis)
        mask *= 2
    pieces = gather_pieces({0: first, 1 << top_bit(): second}, bits)
    return pieces


def reduce_units(array, axis, bits, unit_axis):
    array = reduce_blocks(array, axis, bits, False)
    mask = lax.axis_size("tensor") // 2
    while mask >= 4:
        half = array.shape[unit_axis] // 2
        received = swap_tensor(lax.slice_in_dim(array, half, 2 * half, axis=unit_axis), mask)
        kept = lax.slice_in_dim(array, 0, half, axis=unit_axis)
        array = (kept.astype(F32) + received.astype(F32)).astype(BF)
        mask //= 2
    half = array.shape[axis] // 2
    first = swap_both(lax.slice_in_dim(array, 0, half, axis=axis), (0, 0), (0, 2))
    second = swap_both(
        lax.slice_in_dim(array, half, 2 * half, axis=axis), (1, 0), (1, 2)
    )
    return first.astype(F32) + second.astype(F32)


def gather_rows(own):
    pair = swap_tensor(own, 1)
    mate = swap_halves(swap_wide(own, 1))
    both = swap_halves(swap_wide(pair, 1))
    return jnp.concatenate([pair, both, own, mate], axis=0)


def reduce_rows(far, near):
    rows = far.shape[0] // 2
    far_sum = far[:rows].astype(F32) + swap_halves(swap_wide(far[rows:], 1)).astype(F32)
    moved = swap_tensor(far_sum.astype(BF), 1)
    near_sum = near[:rows].astype(F32) + swap_halves(swap_wide(near[rows:], 1)).astype(F32)
    return near_sum + moved.astype(F32)


def pad_cols(array, width, padded):
    parts = []
    for start in range(0, array.shape[1], width):
        parts.append(jnp.pad(array[:, start : start + width], ((0, 0), (0, padded - width))))
    return jnp.concatenate(parts, axis=1)


def pad_rows(array, width, padded):
    parts = []
    for start in range(0, array.shape[0], width):
        parts.append(jnp.pad(array[start : start + width], ((0, padded - width), (0, 0))))
    return jnp.concatenate(parts, axis=0)


def unpad(array, width, padded, axis):
    parts = [
        lax.slice_in_dim(array, start, start + width, axis=axis)
        for start in range(0, array.shape[axis], padded)
    ]
    return parts[0] if len(parts) == 1 else jnp.concatenate(parts, axis=axis)


def body(
    tokens,
    query_weight,
    key_weight,
    value_weight,
    swish_weight,
    output_weight,
    mlp_gate,
    mlp_up,
    mlp_down,
    gain_one,
    gain_two,
    segments,
    decay_rate,
    cotangent,
):
    wide = lax.axis_size("wide")
    me = lax.axis_index("wide")
    top = top_bit()
    chip_bits = list(range(top))
    numbers = jnp.arange(wide, dtype=jnp.int32)
    index = me ^ (((numbers << 1) & (wide - 1)) | (numbers >> top))
    other = me ^ numbers
    index_back = (other >> 1) | ((other & 1) << top)

    heads = query_weight.shape[1] // KEY
    key_cols = heads * KEY
    val_cols = heads * VAL
    pad_val = heads * PAD

    inputs = permute_blocks(tokens, index).astype(F32)
    gains = permute_blocks(jnp.stack([gain_one, gain_two]), index)
    first_gain, second_gain = gains[0], gains[1]
    scale_one = lax.rsqrt(jnp.mean(inputs * inputs, axis=-1, keepdims=True) + 1e-06)
    normed_local = (inputs * scale_one * first_gain).astype(BF)
    normed = lax.all_gather(normed_local, "tensor", axis=0, tiled=True)
    total = normed.shape[0]

    qk_pieces = gather_pieces({0: jnp.concatenate([query_weight, key_weight], axis=1)}, chip_bits + [top])
    vz_pieces = gather_pieces(
        {0: jnp.concatenate([value_weight, swish_weight], axis=1)}, chip_bits[::-1] + [top]
    )
    wo_pieces = gather_pieces({0: output_weight}, chip_bits + [top])
    full_qk = jnp.concatenate(qk_pieces, axis=0)
    full_vz = jnp.concatenate(vz_pieces, axis=0)
    full_qkvz = jnp.concatenate([full_qk, pad_cols(full_vz, VAL, PAD)], axis=1)
    full_output = pad_rows(jnp.concatenate(wo_pieces, axis=1), VAL, PAD)

    gate_pieces = gather_units(mlp_gate, 1, chip_bits)
    up_pieces = gather_units(mlp_up, 1, chip_bits[::-1])
    down_pieces = gather_units(mlp_down, 0, chip_bits)
    units = gate_pieces[0].shape[1]
    unit_pad = round_up(units, 128)
    full_gate_up = jnp.concatenate(
        [
            jnp.pad(jnp.concatenate(gate_pieces, axis=0), ((0, 0), (0, unit_pad - units))),
            jnp.pad(jnp.concatenate(up_pieces, axis=0), ((0, 0), (0, unit_pad - units))),
        ],
        axis=1,
    )
    full_down = jnp.pad(jnp.concatenate(down_pieces, axis=1), ((0, unit_pad - units), (0, 0)))

    split = 2 * key_cols + pad_val
    qkv = jnp.dot(normed, full_qkvz[:, :split], preferred_element_type=F32).astype(BF)
    gate_pre = jnp.dot(normed, full_qkvz[:, split:], preferred_element_type=F32)
    seg_row = segments
    seg_col = segments.reshape(total, 1)
    gated, mixed = retain_forward(qkv, gate_pre, seg_row, seg_col, decay_rate)
    projected = jnp.dot(gated, full_output, preferred_element_type=F32).astype(BF)
    middle = inputs + lax.psum_scatter(
        projected, "tensor", scatter_dimension=0, tiled=True
    ).astype(F32)

    upstream_rows = permute_blocks(cotangent, index)
    down_rows = gather_rows(upstream_rows)
    hidden_grad = jnp.einsum("nd,fd->nf", down_rows, full_down, preferred_element_type=F32)
    scale_two = lax.rsqrt(jnp.mean(middle * middle, axis=-1, keepdims=True) + 1e-06)
    normed_two = gather_rows((middle * scale_two * second_gain).astype(BF))
    both = jnp.dot(normed_two, full_gate_up, preferred_element_type=F32)
    gate_mlp, up_mlp = both[:, :unit_pad], both[:, unit_pad:]
    gelu_value, gelu_back = jax.vjp(partial(jax.nn.gelu, approximate=True), gate_mlp)
    hidden = (gelu_value * up_mlp).astype(BF)
    unit_grads = jnp.concatenate(
        [gelu_back(hidden_grad * up_mlp)[0].astype(BF), (hidden_grad * gelu_value).astype(BF)],
        axis=1,
    )
    half = unit_grads.shape[0] // 2
    far_grad = jnp.einsum(
        "nf,df->nd", unit_grads[:half], full_gate_up, preferred_element_type=F32
    ).astype(BF)
    near_grad = jnp.einsum(
        "nf,df->nd", unit_grads[half:], full_gate_up, preferred_element_type=F32
    ).astype(BF)
    normed_two_grad = reduce_rows(far_grad, near_grad)
    gain_two_part = jnp.sum(normed_two_grad * middle * scale_two, axis=0)
    inner_two = jnp.mean(normed_two_grad * second_gain * middle, axis=-1, keepdims=True)
    middle_grad = (
        upstream_rows.astype(F32)
        + scale_two * second_gain * normed_two_grad
        - middle * scale_two * scale_two * scale_two * inner_two
    )

    branch_rows = lax.all_gather(middle_grad.astype(BF), "tensor", axis=0, tiled=True)

    out_part = jnp.dot(hidden, full_down, preferred_element_type=F32).astype(BF)
    result = middle + reduce_rows(out_part[:half], out_part[half:])
    layer_out = permute_blocks(result.astype(BF), index_back)

    grad_gate_up = jnp.einsum(
        "na,nb->ab", normed_two, unit_grads, preferred_element_type=F32
    ).astype(BF)
    grad_down = jnp.einsum("na,nb->ab", hidden, down_rows, preferred_element_type=F32).astype(BF)
    gate_sum = reduce_units(grad_gate_up[:, :units], 0, chip_bits[::-1], 1)
    up_sum = reduce_units(grad_gate_up[:, unit_pad : unit_pad + units], 0, chip_bits, 1)
    down_sum = reduce_units(grad_down[:units], 1, chip_bits[::-1], 0)

    gated_grad = jnp.einsum("nd,vd->nv", branch_rows, full_output, preferred_element_type=F32)
    dq, dk, dv, dz = retain_backward(qkv, gate_pre, mixed, gated_grad, seg_row, seg_col, decay_rate)
    all_rows = jnp.concatenate([dq, dk, dv, dz], axis=1)
    total_term = jnp.einsum(
        "nf,df->nd", all_rows, full_qkvz, preferred_element_type=F32
    ).astype(BF)
    normed_grad = lax.psum_scatter(
        total_term, "tensor", scatter_dimension=0, tiled=True
    ).astype(F32)

    grad_output = jnp.einsum("na,nb->ab", gated, branch_rows, preferred_element_type=F32).astype(BF)
    output_sum = reduce_blocks(
        unpad(grad_output, VAL, PAD, 0), 1, [top] + chip_bits[::-1], True
    )
    grad_all = jnp.einsum("na,nb->ab", normed, all_rows, preferred_element_type=F32).astype(BF)
    qk_sum = reduce_blocks(grad_all[:, : 2 * key_cols], 0, [top] + chip_bits[::-1], True)
    vz_sum = reduce_blocks(
        unpad(grad_all[:, 2 * key_cols :], VAL, PAD, 1), 0, [top] + chip_bits, True
    )

    gain_one_part = jnp.sum(normed_grad * inputs * scale_one, axis=0)
    inner_one = jnp.mean(normed_grad * first_gain * inputs, axis=-1, keepdims=True)
    input_grad = (
        middle_grad
        + scale_one * first_gain * normed_grad
        - inputs * scale_one * scale_one * scale_one * inner_one
    )
    input_grad = permute_blocks(input_grad, index_back)
    gain_parts = permute_blocks(jnp.stack([gain_one_part, gain_two_part]), index_back)
    gain_sums = lax.psum(gain_parts, ("wide", "tensor"))
    return (
        layer_out,
        input_grad,
        qk_sum[:, :key_cols],
        qk_sum[:, key_cols:],
        vz_sum[:, :val_cols],
        vz_sum[:, val_cols:],
        output_sum,
        gate_sum,
        up_sum,
        down_sum,
        gain_sums[0],
        gain_sums[1],
    )


def solution(mesh):
    tokens_at = P(("wide", "tensor"), None)
    by_rows = P("wide", "tensor")
    by_cols = P("tensor", "wide")
    in_specs = (
        tokens_at,
        by_rows,
        by_rows,
        by_rows,
        by_rows,
        by_cols,
        by_rows,
        by_rows,
        by_cols,
        P(),
        P(),
        P("wide", None),
        P("tensor"),
        tokens_at,
    )
    out_specs = (
        tokens_at,
        tokens_at,
        by_rows,
        by_rows,
        by_rows,
        by_rows,
        by_cols,
        by_rows,
        by_rows,
        by_cols,
        P(),
        P(),
    )
    return jax.shard_map(body, mesh=mesh, in_specs=in_specs, out_specs=out_specs, check_vma=False)
```

```python
from functools import partial

import jax
import jax.numpy as jnp
from jax import lax
from jax.experimental import pallas as pl
from jax.experimental.pallas import tpu as pltpu
from jax.sharding import PartitionSpec as P

KEY = 256
VAL = 432
BF = jnp.bfloat16
F32 = jnp.float32
VMEM_LIMIT = 56 * 1024 * 1024
COST = 1e8


def round_up(count, step):
    return -(-count // step) * step


def dot_nt(left, right):
    return lax.dot_general(left, right, (((1,), (1,)), ((), ())), preferred_element_type=F32)


def dot_tn(left, right):
    return lax.dot_general(left, right, (((0,), (0,)), ((), ())), preferred_element_type=F32)


def dot_nn(left, right):
    return lax.dot_general(left, right, (((1,), (0,)), ((), ())), preferred_element_type=F32)


def params():
    return pltpu.CompilerParams(vmem_limit_bytes=VMEM_LIMIT)


def cost(micros):
    return pl.CostEstimate(flops=int(micros * COST), transcendentals=0, bytes_accessed=1000)


def row_scale(rows):
    return lax.rsqrt(jnp.mean(rows * rows, axis=-1, keepdims=True) + 1e-06)


def to_own_order(index, source, target, count, width):
    for j in range(count):
        place = pl.ds(pl.multiple_of(index[j] * width, width), width)
        target[:, j * width : (j + 1) * width] = source[:, place]


def to_array_order(index, value, target, count, width):
    for j in range(count):
        place = pl.ds(pl.multiple_of(index[j] * width, width), width)
        target[:, place] = value[:, j * width : (j + 1) * width]


def entry_kernel(count, width, index, tokens, gains, rows, normed, own_gains):
    to_own_order(index, tokens, rows, count, width)
    to_own_order(index, gains, own_gains, count, width)
    value = rows[...].astype(F32)
    normed[...] = (value * row_scale(value) * own_gains[0:1, :]).astype(BF)


def row_call(kernel, name, index, ins, outs, waits=()):
    total = max(a.shape[0] for a in ins)
    chunk = min(128, total)

    def spec(a):
        if a.shape[0] == total:
            return (chunk, a.shape[1]), lambda i, index: (i, 0)
        return a.shape, lambda i, index: (0, 0)

    return call(
        kernel,
        name,
        [(a, *spec(a)) for a in ins],
        [(a.shape, a.dtype, *spec(a)) for a in outs],
        (total // chunk,),
        waits=waits,
        table=index,
    )


def like(array, dtype):
    return jax.ShapeDtypeStruct(array.shape, dtype)


def order_kernel(count, width, index, source, target):
    to_own_order(index, source, target, count, width)


def middle_kernel(index, rows, moved, gains, middle, normed):
    value = rows[...].astype(F32) + moved[...].astype(F32)
    middle[...] = value
    normed[...] = (value * row_scale(value) * gains[1:2, :]).astype(BF)


def norm_back(rows, gain, upstream):
    scale = row_scale(rows)
    inner = jnp.mean(upstream * gain * rows, axis=-1, keepdims=True)
    part = jnp.sum(upstream * rows * scale, axis=0, keepdims=True)
    return scale * gain * upstream - rows * scale * scale * scale * inner, part


def middle_back_kernel(index, near, mate, moved, middle, upstream, gains, grad, low, part):
    @pl.when(pl.program_id(0) == 0)
    def _():
        part[...] = jnp.zeros_like(part)

    total = near[...].astype(F32) + mate[...].astype(F32) + moved[...].astype(F32)
    back, gain_part = norm_back(middle[...], gains[1:2, :], total)
    value = upstream[...].astype(F32) + back
    grad[...] = value
    low[...] = value.astype(BF)
    part[...] += gain_part


def out_kernel(count, width, index, near, mate, moved, middle, target):
    total = near[...].astype(F32) + mate[...].astype(F32) + moved[...].astype(F32)
    value = (middle[...] + total).astype(BF)
    to_array_order(index, value, target, count, width)


def final_kernel(count, width, index, moved, rows, grad, gains, part_two, target, parts):
    @pl.when(pl.program_id(0) == 0)
    def _():
        parts[...] = jnp.zeros_like(parts)
        to_array_order(index, part_two[...], parts.at[1:2, :], count, width)

    back, gain_part = norm_back(rows[...].astype(F32), gains[0:1, :], moved[...].astype(F32))
    to_array_order(index, grad[...] + back, target, count, width)
    for j in range(count):
        place = pl.ds(pl.multiple_of(index[j] * width, width), width)
        parts[0:1, place] += gain_part[:, j * width : (j + 1) * width]


def call(kernel, name, ins, outs, grid, scratch=(), waits=(), table=None, micros=5):
    ranks = len(grid)

    def spec(shape, block, index):
        if block is None:
            zeros = (0,) * len(shape)
            return pl.BlockSpec(shape, lambda *at: zeros, pipeline_mode=pl.Buffered(1))
        return pl.BlockSpec(block, index)

    def out_spec(shape, block, index):
        if block is None:
            zeros = (0,) * len(shape)
            return pl.BlockSpec(shape, lambda *at: zeros)
        return pl.BlockSpec(block, index)

    first = 0 if table is None else 1
    count = len(ins)

    def run(*refs):
        kernel(*refs[: first + count], *refs[first + count + len(waits) :])

    return pl.pallas_call(
        run,
        grid_spec=pltpu.PrefetchScalarGridSpec(
            num_scalar_prefetch=first,
            grid=grid,
            in_specs=[spec(x.shape, b, m) for x, b, m in ins]
            + [pl.BlockSpec(memory_space=pl.ANY)] * len(waits),
            out_specs=[out_spec(sh, b, m) for sh, _, b, m in outs],
            scratch_shapes=list(scratch),
        ),
        out_shape=[jax.ShapeDtypeStruct(sh, dt) for sh, dt, _, _ in outs],
        compiler_params=params(),
        cost_estimate=cost(micros),
        name=name,
    )(*(() if table is None else (table,)), *(x for x, _, _ in ins), *waits)


def put(target, at, value):
    target[:, at : at + value.shape[1]] = value
    return at + value.shape[1]


def fill(target, at, end):
    if end > at:
        target[:, at:end] = jnp.zeros((target.shape[0], end - at), BF)
    return end


def pack_kernel(q, k, v, z, wo, gate, up, down, first, second, third, fourth):
    at = 0
    for part in (q, k, v):
        at = put(first, at, part[...])
    fill(first, at, first.shape[1])
    for left, right, target in ((z, wo, second), (up, down, third)):
        at = put(target, 0, left[...])
        at = fill(target, at, target.shape[1] // 2)
        at = put(target, at, right[...].T)
        fill(target, at, target.shape[1])
    at = put(fourth, 0, gate[...])
    fill(fourth, at, fourth.shape[1])


def pack(q, k, v, z, wo, gate, up, down):
    rows = q.shape[0]
    cols = round_up(q.shape[1] + k.shape[1] + v.shape[1], 128)
    widths = [cols] + [2 * round_up(x.shape[1], 128) for x in (z, up)] + [round_up(gate.shape[1], 128)]
    return call(
        pack_kernel,
        "pack",
        [(x, None, None) for x in (q, k, v, z, wo, gate, up, down)],
        [((rows, w), BF, None, None) for w in widths],
        (1,),
    )


def join(pieces, cols=slice(None)):
    return jnp.concatenate([p[:, cols] for p in pieces], axis=0)


def project_kernel(count, tiles, normed, *refs):
    first, second, qkv, z = refs[:count], refs[count : 2 * count], refs[-2], refs[-1]
    at = pl.program_id(0)

    @pl.when(at < tiles)
    def _():
        qkv[...] = dot_nn(normed[...], join(first)).astype(BF)

    @pl.when(at >= tiles)
    def _():
        z[...] = dot_nn(normed[...], join(second))


def project(normed, first, second, cols, val_cols, waits):
    total = normed.shape[0]
    width = first[0].shape[0]
    tile = 256
    tiles, more = pl.cdiv(cols, tile), pl.cdiv(val_cols, tile)
    in_first = lambda i: (0, jnp.minimum(i, tiles - 1))
    in_second = lambda i: (0, jnp.maximum(i - tiles, 0))
    return call(
        partial(project_kernel, len(first), tiles),
        "project",
        [(normed, None, None)]
        + [(p, (width, tile), in_first) for p in first]
        + [(p, (width, tile), in_second) for p in second],
        [
            ((total, cols), BF, (total, tile), in_first),
            ((total, val_cols), F32, (total, tile), in_second),
        ],
        (tiles + more,),
        waits=waits,
        micros=21,
    )


def right_part(pieces, cols):
    block = (pieces[0].shape[0], round_up(cols, 128))
    return [(p, block, lambda *i: (0, 1)) for p in pieces]


def left_part(pieces, cols):
    block = (pieces[0].shape[0], min(round_up(cols, 128), pieces[0].shape[1]))
    return [(p, block, lambda *i: (0, 0)) for p in pieces]


def spread_kernel(width, groups, *refs):
    values, at = [], 0
    for lefts, _ in groups:
        values.append(jnp.concatenate([r[...] for r in refs[at : at + lefts]], axis=1))
        at += lefts
    target = refs[-1]
    for j in range(groups[0][1]):
        total = None
        for i, (value, (_, count)) in enumerate(zip(values, groups)):
            part = dot_nt(value, refs[at + i * count + j][:, : value.shape[1]])
            total = part if total is None else total + part
        target[:, j * width : (j + 1) * width] = total.astype(target.dtype)


def spread(name, pairs, micros, waits=()):
    total = pairs[0][0][0].shape[0]
    count = len(pairs[0][1])
    width = pairs[0][1][0][1][0]
    block = min(512, total)
    return call(
        partial(spread_kernel, width, [(len(lefts), count) for lefts, _ in pairs]),
        name,
        [(x, (block, x.shape[1]), lambda i: (i, 0)) for lefts, _ in pairs for x in lefts]
        + [spec for _, specs in pairs for spec in specs],
        [((total, width * count), BF, (block, width * count), lambda i: (i, 0))],
        (total // block,),
        waits=waits,
        micros=micros,
    )[0]


def spread_rows_kernel(width, groups, *refs):
    own, mate = refs[-2], refs[-1]
    count = groups[0][1]
    lefts, sets = refs[: len(groups)], refs[len(groups) : -2]
    values = [left[...] for left in lefts]
    rows = own.shape[0]
    for j in range(count):
        total = None
        for i, (cols, _) in enumerate(groups):
            part = dot_nt(values[i], sets[i * count + j][:, :cols])
            total = part if total is None else total + part
        total = total.astype(BF)
        turned = (j + count // 2) % count
        own[:, j * width : (j + 1) * width] = total[:rows]
        mate[:, turned * width : (turned + 1) * width] = total[rows:]


def spread_rows(name, pairs, waits=()):
    total = pairs[0][0].shape[0]
    count = len(pairs[0][1])
    width = pairs[0][1][0][1][0]
    shape = (total // 2, width * count)
    return call(
        partial(spread_rows_kernel, width, [(x.shape[1], count) for x, _ in pairs]),
        name,
        [(x, None, None) for x, _ in pairs] + [spec for _, specs in pairs for spec in specs],
        [(shape, BF, None, None)] * 2,
        (1,),
        waits=waits,
    )


def hidden_kernel(cols, steps, own, mate, *refs):
    pieces, target = refs[:-1], refs[-1]
    at = pl.program_id(0)
    half = len(pieces) // 2

    @pl.when(at < steps)
    def _():
        target[...] = dot_nn(own[...], join(pieces, slice(0, cols)))

    @pl.when(at >= steps)
    def _():
        turned = pieces[half:] + pieces[:half]
        target[...] = dot_nn(mate[...], join(turned, slice(0, cols)))


def hidden_side(own, mate, pieces, cols, waits=()):
    rows, features = own.shape
    block = min(256, rows)
    steps = rows // block
    return call(
        partial(hidden_kernel, cols, steps),
        "hidden_side",
        [
            (own, (block, features), lambda i: (jnp.minimum(i, steps - 1), 0)),
            (mate, (block, features), lambda i: (jnp.maximum(i - steps, 0), 0)),
        ]
        + right_part(pieces, cols),
        [((2 * rows, cols), F32, (block, cols), lambda i: (i, 0))],
        (2 * steps,),
        waits=waits,
    )[0]


def units_kernel(count, own, mate, grad, *refs):
    gates, ups = refs[:count], refs[count : 2 * count]
    hidden, gate_grad, up_grad = refs[2 * count :]
    rows = own.shape[0]
    half = count // 2
    for source, turn, place in ((own, 0, slice(0, rows)), (mate, half, slice(rows, 2 * rows))):
        value = source[...]
        a = dot_nn(value, join(gates[turn:] + gates[:turn]))
        b = dot_nn(value, join(ups[turn:] + ups[:turn]))
        inner = 0.7978845608028654 * (a + 0.044715 * (a * a * a))
        tanh = jnp.tanh(inner)
        cdf = 0.5 * (1.0 + tanh)
        gelu = a * cdf
        slope = cdf + 0.5 * a * (1.0 - tanh * tanh) * 0.7978845608028654 * (
            1.0 + 3.0 * 0.044715 * (a * a)
        )
        dh = grad[place, :]
        hidden[place, :] = (gelu * b).astype(BF)
        gate_grad[place, :] = (dh * b * slope).astype(BF)
        up_grad[place, :] = (dh * gelu).astype(BF)


def unit_rows(own, mate, gates, ups, grad, waits=()):
    rows, features = own.shape
    units = grad.shape[1]
    width = gates[0].shape[0]
    tile = min(256, units)
    by_tile = lambda j: (0, j)
    return call(
        partial(units_kernel, len(gates)),
        "unit_rows",
        [(own, None, None), (mate, None, None), (grad, (2 * rows, tile), by_tile)]
        + [(p, (width, tile), by_tile) for p in (*gates, *ups)],
        [((2 * rows, units), BF, (2 * rows, tile), by_tile)] * 3,
        (pl.cdiv(units, tile),),
        waits=waits,
        micros=10,
    )


def grads_kernel(half, rows, table, *refs):
    lefts, rights = refs[: half * len(rows)], refs[half * len(rows) : -2]
    away, kept = refs[-2], refs[-1]
    total = None
    for i, (which, start) in enumerate(rows):
        blocks = lefts[i * half : (i + 1) * half]
        left = jnp.concatenate([b[...] for b in blocks], axis=1)
        part = dot_tn(left, rights[which][start : start + left.shape[0], :])
        total = part if total is None else total + part
    width = away.shape[1]
    at = pl.program_id(0)
    for target, here in ((away, at == 0), (kept, at == 1)):

        @pl.when(here)
        def _():
            for j in range(half):
                value = total[j * width : (j + 1) * width].astype(BF)
                fill(target.at[j], put(target.at[j], 0, value), target.shape[2])


def weight_grads(name, lefts, rights, bits, waits=()):
    count = lax.axis_size("wide")
    half = count // 2
    features = lefts[0][0].shape[1]
    width = features // count
    order = sorted(range(count), key=lambda j: tuple(j >> b & 1 for b in bits) + (j,))
    table = jnp.array(order[half:] + order[:half], jnp.int32)
    cols = round_up(rights[0].shape[1], 128)

    def place(j, turned):
        if turned:
            return lambda s, table: (0, jnp.bitwise_xor(table[s * half + j], half))
        return lambda s, table: (0, table[s * half + j])

    return call(
        partial(grads_kernel, half, [(which, start) for _, _, which, start in lefts]),
        name,
        [
            (x, (x.shape[0], width), place(j, turned))
            for x, turned, _, _ in lefts
            for j in range(half)
        ]
        + [(x, None, None) for x in rights],
        [((half, width, cols), BF, None, None)] * 2,
        (2,),
        waits=waits,
        table=table,
        micros=7,
    )


def branch_kernel(heads, cols, rows, z, mixed, *refs):
    pieces, dz, down = refs[:-2], refs[-2], refs[-1]
    dy = dot_nn(rows[...], join(pieces, slice(0, cols)))
    for h in range(heads):
        at = slice(h * VAL, (h + 1) * VAL)
        grouped, inverse = normalize(mixed[h])
        gate, upstream = z[:, at], dy[:, at]
        sig = jax.nn.sigmoid(gate)
        dz[:, at] = (upstream * grouped * (sig + gate * sig * (1.0 - sig))).astype(BF)
        dg = upstream * (gate * sig)
        first = jnp.mean(dg, axis=-1, keepdims=True)
        second = jnp.mean(dg * grouped, axis=-1, keepdims=True)
        down[h] = (inverse * (dg - first - grouped * second)).astype(BF)


def branch_back(rows, z, mixed, pieces, waits=()):
    heads, total, _ = mixed.shape
    cols = heads * VAL
    block = min(256, total)
    by_rows = lambda i: (i, 0)
    by_heads = lambda i: (0, i, 0)
    return call(
        partial(branch_kernel, heads, cols),
        "branch_back",
        [
            (rows, (block, rows.shape[1]), by_rows),
            (z, (block, cols), by_rows),
            (mixed, (heads, block, VAL), by_heads),
        ]
        + right_part(pieces, cols),
        [
            ((total, cols), BF, (block, cols), by_rows),
            ((heads, total, VAL), BF, (heads, block, VAL), by_heads),
        ],
        (total // block,),
        waits=waits,
        micros=12,
    )


def weight_block(rate, row_seg, col_seg, offset, block):
    down = lax.broadcasted_iota(jnp.int32, (block, block), 0)
    across = lax.broadcasted_iota(jnp.int32, (block, block), 1)
    gap = offset + down - across
    allowed = (gap >= 0) & (row_seg == col_seg)
    return jnp.where(allowed, jnp.exp(-rate * jnp.maximum(gap, 0).astype(F32)), 0.0)


def normalize(mixed):
    centred = mixed - jnp.mean(mixed, axis=-1, keepdims=True)
    inverse = lax.rsqrt(jnp.mean(centred * centred, axis=-1, keepdims=True) + 1.0)
    return centred * inverse, inverse


def forward_kernel(block, steps, heads, rate, seg_col, seg_row, qkv, z, gated, mixed, values, acc):
    at = pl.program_id(0)
    rows = pl.ds(pl.multiple_of(at * block, block), block)
    key_at, val_at = heads * KEY, 2 * heads * KEY

    @pl.when(at == 0)
    def _():
        for h in range(heads):
            values[h] = qkv[:, val_at + h * VAL : val_at + (h + 1) * VAL]

    acc[...] = jnp.zeros_like(acc)
    for step in range(steps):

        @pl.when(step <= at)
        def _():
            cols = pl.ds(step * block, block)
            for h in range(heads):
                weight = weight_block(
                    rate[0:1, h : h + 1], seg_col[...], seg_row[:, cols], (at - step) * block, block
                )
                q = qkv[rows, h * KEY : (h + 1) * KEY]
                k = qkv[cols, key_at + h * KEY : key_at + (h + 1) * KEY]
                probs = (dot_nt(q, k) * weight).astype(BF)
                acc[h] += dot_nn(probs, values[h, cols, :])

    for h in range(heads):
        total = acc[h]
        grouped, _ = normalize(total)
        mixed[h] = total
        gate = z[:, h * VAL : (h + 1) * VAL]
        gated[:, h * VAL : (h + 1) * VAL] = (gate * jax.nn.sigmoid(gate) * grouped).astype(BF)


def retain_forward(qkv, z, seg_row, seg_col, rate, waits=()):
    total = qkv.shape[0]
    heads = rate.shape[1]
    block = min(256, total)
    steps = total // block
    by_rows = lambda i: (i, 0)
    by_heads = lambda i: (0, i, 0)
    return call(
        partial(forward_kernel, block, steps, heads),
        "retain_forward",
        [
            (rate, None, None),
            (seg_col, (block, 1), by_rows),
            (seg_row, None, None),
            (qkv, None, None),
            (z, (block, heads * VAL), by_rows),
        ],
        [
            ((total, heads * VAL), BF, (block, heads * VAL), by_rows),
            ((heads, total, VAL), F32, (heads, block, VAL), by_heads),
        ],
        (steps,),
        [pltpu.VMEM((heads, total, VAL), BF), pltpu.VMEM((heads, block, VAL), F32)],
        waits,
        micros=12,
    )


def backward_kernel(
    block, steps, heads, rate, seg_col, seg_row, qkv, down, grads, val_grads, values, dk_acc, dv_acc, dq_acc
):
    at = pl.program_id(0)
    rows = pl.ds(pl.multiple_of(at * block, block), block)
    key_at, val_at = heads * KEY, 2 * heads * KEY

    @pl.when(at == 0)
    def _():
        dk_acc[...] = jnp.zeros_like(dk_acc)
        dv_acc[...] = jnp.zeros_like(dv_acc)
        for h in range(heads):
            values[h] = qkv[:, val_at + h * VAL : val_at + (h + 1) * VAL]

    dq_acc[...] = jnp.zeros_like(dq_acc)
    for step in range(steps):

        @pl.when(step <= at)
        def _():
            cols = pl.ds(step * block, block)
            for h in range(heads):
                weight = weight_block(
                    rate[0:1, h : h + 1], seg_col[...], seg_row[:, cols], (at - step) * block, block
                )
                q = qkv[rows, h * KEY : (h + 1) * KEY]
                k = qkv[cols, key_at + h * KEY : key_at + (h + 1) * KEY]
                probs = (dot_nt(q, k) * weight).astype(BF)
                score_grad = (dot_nt(down[h], values[h, cols, :]) * weight).astype(BF)
                dq_acc[h] += dot_nn(score_grad, k)
                dk_acc[h, cols, :] += dot_tn(score_grad, q)
                dv_acc[h, cols, :] += dot_tn(probs, down[h])

    for h in range(heads):
        grads[rows, h * KEY : (h + 1) * KEY] = dq_acc[h].astype(BF)

    @pl.when(at == steps - 1)
    def _():
        for h in range(heads):
            grads[:, key_at + h * KEY : key_at + (h + 1) * KEY] = dk_acc[h].astype(BF)
            val_grads[:, h * VAL : (h + 1) * VAL] = dv_acc[h].astype(BF)


def retain_backward(qkv, down, seg_row, seg_col, rate, waits=()):
    total = qkv.shape[0]
    heads = rate.shape[1]
    block = min(256, total)
    steps = total // block
    return call(
        partial(backward_kernel, block, steps, heads),
        "retain_backward",
        [
            (rate, None, None),
            (seg_col, (block, 1), lambda i: (i, 0)),
            (seg_row, None, None),
            (qkv, None, None),
            (down, (heads, block, VAL), lambda i: (0, i, 0)),
        ],
        [((total, 2 * heads * KEY), BF, None, None), ((total, heads * VAL), BF, None, None)],
        (steps,),
        [
            pltpu.VMEM((heads, total, VAL), BF),
            pltpu.VMEM((heads, total, KEY), F32),
            pltpu.VMEM((heads, total, VAL), F32),
            pltpu.VMEM((heads, block, KEY), F32),
        ],
        waits,
        micros=17,
    )


def swap_wide(array, mask):
    count = lax.axis_size("wide")
    return lax.ppermute(array, "wide", [(i, i ^ mask) for i in range(count)])


def swap_tensor(array, mask):
    count = lax.axis_size("tensor")
    return lax.ppermute(array, "tensor", [(i, i ^ mask) for i in range(count)])


def top_bit():
    return lax.axis_size("wide").bit_length() - 2


def mask_of(bit):
    return 1 if bit == top_bit() else 2 << bit


def double(first, second, bits, cores, sync, late=()):
    top = 1 << top_bit()
    mates_first, mates_second = {}, {}
    new = (0, 0)

    def to_mates(sync):
        mates_first[new[0] | top] = swap_wide(first[new[0]], 1)
        mates_second[new[1] | top] = swap_wide(second[new[1]], 1)
        return (mates_first[new[0] | top], mates_second[new[1] | top])

    for place, (bit_first, bit_second) in enumerate(bits):
        count = len(first)
        for step, (one, two) in enumerate(zip(list(first), list(second))):
            if place == len(bits) - 1 and step == count - 1:
                sync = (*sync, *late)
            sent = after((first[one], second[two]), *sync) if sync else (first[one], second[two])
            sync = to_mates(sync) if cores else ()
            new = (one | 1 << bit_first, two | 1 << bit_second)
            first[new[0]] = swap_wide(sent[0], mask_of(bit_first))
            second[new[1]] = swap_wide(sent[1], mask_of(bit_second))
            sync = (first[new[0]], second[new[1]], *sync)
    if cores:
        sync = to_mates(sync)
        first.update(mates_first)
        second.update(mates_second)
    return sync


def listed(pieces):
    return [pieces[number] for number in range(len(pieces))]


def choose(even, left, right):
    return jnp.where(even, left, right), jnp.where(even, right, left)


def exchange_units(block, got, even):
    own, given = choose(even, block, got)
    return {0: own}, {0: swap_wide(given, 1)}


def widen_units(pieces, cols, parts):
    mask = 4
    while mask < lax.axis_size("tensor"):
        pieces = {n: beside(p, swap_tensor(p, mask), cols, parts) for n, p in pieces.items()}
        cols *= 2
        mask *= 2
    return pieces


def beside(left, right, cols, parts):
    step = round_up(cols, 128)
    rest = jnp.zeros((left.shape[0], round_up(2 * cols, 128) - 2 * cols), left.dtype)
    out = []
    for i in range(parts):
        at = slice(i * step, i * step + cols)
        out += [left[:, at], right[:, at], rest]
    return jnp.concatenate(out, axis=1)


def fold(kept, got, last):
    half = kept.shape[0] // 2
    dtype = F32 if last else BF

    def add(a, b):
        return (kept[a:b].astype(F32) + got[a:b].astype(F32)).astype(dtype)

    return add(half, 2 * half), add(0, half)


def reduce_rest(away, kept, bits, waits=()):
    for place, bit in enumerate(bits):
        got = swap_wide(away, mask_of(bit))
        if place == len(bits) - 1:
            got = after(got, *waits) if waits else got
            return kept[0].astype(F32) + got[0].astype(F32)
        away, kept = fold(kept, got, False)


def reduce_chip(away, kept, bits, waits):
    for place, bit in enumerate(bits):
        got = swap_wide(away, mask_of(bit))
        if place in waits:
            got = after(got, *waits[place])
        away, kept = fold(kept, got, False)
    return kept[0], away[0]


def reduce_units(own, mate, cols, even):
    mask = lax.axis_size("tensor") // 2
    while mask >= 4:
        cols //= 2
        own, mate = (
            (
                p[:, :cols].astype(F32) + swap_tensor(p[:, cols : 2 * cols], mask).astype(F32)
            ).astype(BF)
            for p in (own, mate)
        )
        mask //= 2
    return choose(even, own, swap_wide(mate, 1))


def add_pair(pair):
    return pair[0].astype(F32) + pair[1].astype(F32)


def after(value, *earlier):
    return lax.optimization_barrier((value, earlier))[0]


def sum_all(array):
    mask = 1
    while mask < lax.axis_size("tensor"):
        array = array + swap_tensor(array, mask)
        mask *= 2
    mask = 1
    while mask < lax.axis_size("wide"):
        array = array + swap_wide(array, mask)
        mask *= 2
    return array


def body(
    tokens,
    query_weight,
    key_weight,
    value_weight,
    swish_weight,
    output_weight,
    mlp_gate,
    mlp_up,
    mlp_down,
    gain_one,
    gain_two,
    segments,
    decay_rate,
    cotangent,
):
    wide = lax.axis_size("wide")
    me = lax.axis_index("wide")
    top = top_bit()
    chip_bits = list(range(top))
    turned = chip_bits[::-1]
    numbers = jnp.arange(wide, dtype=jnp.int32)
    index = me ^ (((numbers << 1) & (wide - 1)) | (numbers >> top))
    features = tokens.shape[1]
    width = features // wide

    heads = query_weight.shape[1] // KEY
    key_cols = heads * KEY
    val_cols = heads * VAL
    own_units = mlp_gate.shape[1]
    rate = decay_rate.reshape(1, heads)

    rows, normed_local, gains = row_call(
        partial(entry_kernel, wide, width),
        "entry",
        index,
        [tokens, jnp.stack([gain_one, gain_two])],
        [like(tokens, BF), like(tokens, BF), jax.ShapeDtypeStruct((2, features), F32)],
    )
    normed = lax.all_gather(normed_local, "tensor", axis=0, tiled=True)
    total = normed.shape[0]

    block_a, block_b, block_u, block_g = pack(
        query_weight,
        key_weight,
        value_weight,
        swish_weight,
        output_weight,
        mlp_gate,
        mlp_up,
        mlp_down,
    )
    even = (me & 1) == 0
    gate_block = swap_tensor(block_g, 2)
    (upstream,) = row_call(
        partial(order_kernel, wide, width), "order", index, [cotangent], [like(cotangent, BF)]
    )
    crossing, opposite = list(zip(chip_bits, turned)), list(zip(turned, chip_bits))
    pieces_a, pieces_b = {0: block_a}, {0: block_b}
    sync = double(pieces_a, pieces_b, crossing, True, (), (gate_block, upstream))
    pieces_a, pieces_b = listed(pieces_a), listed(pieces_b)
    gates_own, gates_mate = exchange_units(block_g, gate_block, even)
    units = own_units * lax.axis_size("tensor") // 4
    gates_own, gates_mate = (widen_units(p, own_units, 1) for p in (gates_own, gates_mate))
    double(gates_own, gates_mate, crossing[:1], False, sync[:2])

    qkv_cols = 2 * key_cols + val_cols
    block_u, upstream_sent = after((block_u, upstream), normed)
    qkv, z = project(normed, pieces_a, pieces_b, qkv_cols, val_cols, (upstream,))
    up_block = swap_tensor(block_u, 2)
    upstream_pair = swap_tensor(upstream_sent, 1)
    seg_row = segments
    seg_col = segments.reshape(total, 1)
    gated, mixed = retain_forward(
        qkv, z, seg_row, seg_col, rate, (*gates_own.values(), *gates_mate.values())
    )
    double(gates_own, gates_mate, crossing[1:], False, (qkv,))
    early = tuple(p[n] for p in (gates_own, gates_mate) for n in list(p)[:-1])
    gates = listed({**gates_own, **{n | 1 << top: p for n, p in gates_mate.items()}})
    up_block = after(up_block, gated)
    projected = spread(
        "project_out",
        [((gated,), right_part(pieces_b, val_cols))],
        8,
        (up_block, upstream_pair, *early),
    )
    moved_up = lax.psum_scatter(projected, "tensor", scatter_dimension=0, tiled=True)

    ups_own, ups_mate = exchange_units(block_u, up_block, even)
    ups_own, ups_mate = (widen_units(p, own_units, 2) for p in (ups_own, ups_mate))
    double(ups_own, ups_mate, opposite, False, ())
    ups = listed({**ups_own, **{n | 1 << top: p for n, p in ups_mate.items()}})
    upstream_mate = swap_wide(upstream, 1)
    upstream_both = swap_wide(upstream_pair, 1)
    near_hidden = hidden_side(upstream, upstream_mate, ups, units)
    middle, normed_two_local = row_call(
        middle_kernel,
        "middle",
        index,
        [rows, moved_up, gains],
        [like(rows, F32), like(rows, BF)],
        (near_hidden,),
    )

    own = normed_two_local
    pair = swap_tensor(own, 1)
    mate = swap_wide(own, 1)
    near = unit_rows(own, mate, gates, ups, near_hidden)

    def input_side(parts, waits=()):
        return spread_rows(
            "input_side",
            [(parts[1], left_part(gates, units)), (parts[2], left_part(ups, units))],
            waits,
        )

    def output_side(parts, waits=()):
        return spread_rows("output_side", [(parts[0], right_part(ups, units))], waits)

    near_own, near_mate = input_side(near)
    far_hidden = hidden_side(upstream_pair, upstream_both, ups, units, (near_own,))
    pair = after(pair, far_hidden)
    both = swap_wide(pair, 1)
    far = unit_rows(pair, both, gates, ups, far_hidden, (near_own,))
    far_own, far_mate = input_side(far)
    far_sent = (far_own.astype(F32) + swap_wide(far_mate, 1).astype(F32)).astype(BF)
    moved_far = swap_tensor(far_sent, 1)
    near_got = swap_wide(near_mate, 1)
    token_rows = own.shape[0]

    def groups(a, b, c, d):
        return [(a, False, 0, 0), (b, True, 0, token_rows), (c, False, 1, 0), (d, True, 1, token_rows)]

    unit_tokens = groups(own, mate, pair, both)
    down_away, down_kept = weight_grads(
        "down_grads",
        groups(upstream, upstream_mate, upstream_pair, upstream_both),
        [near[0], far[0]],
        turned,
        (far_sent,),
    )
    gate_away, gate_kept = weight_grads(
        "gate_grads", unit_tokens, [near[1], far[1]], chip_bits, (down_away,)
    )
    middle_grad, branch_local, gain_two_part = row_call(
        middle_back_kernel,
        "middle_back",
        index,
        [near_own, near_got, moved_far, middle, upstream, gains],
        [like(rows, F32), like(rows, BF), jax.ShapeDtypeStruct((1, features), F32)],
        (gate_away,),
    )
    branch_rows = lax.all_gather(branch_local, "tensor", axis=0, tiled=True)

    up_away, up_kept = weight_grads(
        "up_grads", unit_tokens, [near[2], far[2]], turned, (branch_local,)
    )
    out_far_own, out_far_mate = output_side(far, (up_away,))
    out_near_own, out_near_mate = output_side(near, (up_away,))
    out_sent = (out_far_own.astype(F32) + swap_wide(out_far_mate, 1).astype(F32)).astype(BF)
    out_got = swap_wide(out_near_mate, 1)
    outs = {0: (out_far_own, out_near_own)}
    down_part = reduce_chip(down_away, down_kept, turned, outs)
    gate_part = reduce_chip(gate_away, gate_kept, chip_bits, outs)

    swish_rows, down = branch_back(branch_rows, z, mixed, pieces_b, (out_near_own, out_far_own))
    down_sum, gate_sum = (reduce_units(*p, units, even) for p in (down_part, gate_part))
    up_sum = reduce_units(*reduce_chip(up_away, up_kept, turned, {**outs, top - 1: (swish_rows,)}), units, even)
    down_sum, gate_sum, up_sum = (
        (kept, swap_tensor(after(sent, branch_rows), 2))
        for kept, sent in (down_sum, gate_sum, up_sum)
    )
    out_moved = swap_tensor(after(out_sent, branch_rows), 1)
    qk_rows, v_rows = retain_backward(qkv, down, seg_row, seg_col, rate)

    def whole_grads(name, left, right, bits, waits):
        return weight_grads(name, [(left, False, 0, 0)], [right], bits, waits)

    order_a, order_b = [top] + turned, [top] + chip_bits
    swish_parts = whole_grads("swish_grads", normed, swish_rows, order_b, (v_rows,))
    out_parts = whole_grads("out_grads", branch_rows, gated, order_a, (swish_parts[0],))
    total_term = spread(
        "normed_grad",
        [
            ((qk_rows, v_rows), left_part(pieces_a, qkv_cols)),
            ((swish_rows,), left_part(pieces_b, val_cols)),
        ],
        17,
        (out_parts[0],),
    )
    total_term = after(total_term, down_sum[1], gate_sum[1], up_sum[1], out_moved)
    moved_down = lax.psum_scatter(total_term, "tensor", scatter_dimension=0, tiled=True)
    qk_parts = whole_grads("qk_grads", normed, qk_rows, order_a, (total_term,))
    v_parts = whole_grads("v_grads", normed, v_rows, order_b, (qk_parts[0],))
    (layer_out,) = row_call(
        partial(out_kernel, wide, width),
        "layer_out",
        index,
        [out_near_own, out_got, out_moved, middle],
        [like(rows, BF)],
        (v_parts[0],),
    )
    input_grad, gain_parts = row_call(
        partial(final_kernel, wide, width),
        "final",
        index,
        [moved_down, rows, middle_grad, gains, gain_two_part],
        [like(rows, F32), jax.ShapeDtypeStruct((2, features), F32)],
        (layer_out,),
    )
    swish_sum = reduce_rest(*swish_parts, order_b, (gain_parts,))
    output_sum = reduce_rest(*out_parts, order_a, (gain_parts,))
    qk_sum = reduce_rest(*qk_parts, order_a, (gain_parts,))
    v_sum = reduce_rest(*v_parts, order_b, (gain_parts,))
    gain_sums = sum_all(gain_parts)
    return (
        layer_out,
        input_grad,
        qk_sum[:, :key_cols],
        qk_sum[:, key_cols:],
        v_sum[:, :val_cols],
        swish_sum[:, :val_cols],
        output_sum[:, :val_cols].T,
        add_pair(gate_sum)[:, :own_units],
        add_pair(up_sum)[:, :own_units],
        add_pair(down_sum)[:, :own_units].T,
        gain_sums[0],
        gain_sums[1],
    )


def solution(mesh):
    tokens_at = P(("wide", "tensor"), None)
    by_rows = P("wide", "tensor")
    by_cols = P("tensor", "wide")
    in_specs = (
        tokens_at,
        by_rows,
        by_rows,
        by_rows,
        by_rows,
        by_cols,
        by_rows,
        by_rows,
        by_cols,
        P(),
        P(),
        P("wide", None),
        P("tensor"),
        tokens_at,
    )
    out_specs = (
        tokens_at,
        tokens_at,
        by_rows,
        by_rows,
        by_rows,
        by_rows,
        by_cols,
        by_rows,
        by_rows,
        by_cols,
        P(),
        P(),
    )
    return jax.shard_map(body, mesh=mesh, in_specs=in_specs, out_specs=out_specs, check_vma=False)
```

```python
from functools import partial

import jax
import jax.numpy as jnp
from jax import lax
from jax.experimental import pallas as pl
from jax.experimental.layout import Layout, with_layout_constraint
from jax.experimental.pallas import tpu as pltpu
from jax.sharding import PartitionSpec as P

KEY = 256
VAL = 432
BF = jnp.bfloat16
F32 = jnp.float32
VMEM_LIMIT = 56 * 1024 * 1024


def round_up(count, step):
    return -(-count // step) * step


def lanes(count):
    return round_up(count, 128)


def dot_nt(left, right):
    return lax.dot_general(left, right, (((1,), (1,)), ((), ())), preferred_element_type=F32)


def dot_tn(left, right):
    return lax.dot_general(left, right, (((0,), (0,)), ((), ())), preferred_element_type=F32)


def dot_nn(left, right):
    return lax.dot_general(left, right, (((1,), (0,)), ((), ())), preferred_element_type=F32)


def params():
    return pltpu.CompilerParams(vmem_limit_bytes=VMEM_LIMIT)


def cost():
    return pl.CostEstimate(flops=1000000, transcendentals=0, bytes_accessed=0)


def row_scale(rows):
    return lax.rsqrt(jnp.mean(rows * rows, axis=-1, keepdims=True) + 1e-06)


def to_own_order(index, source, target, count, width):
    for j in range(count):
        place = pl.ds(pl.multiple_of(index[j] * width, width), width)
        target[:, j * width : (j + 1) * width] = source[:, place]


def to_array_order(index, value, target, count, width):
    for j in range(count):
        place = pl.ds(pl.multiple_of(index[j] * width, width), width)
        target[:, place] = value[:, j * width : (j + 1) * width]


def entry_kernel(count, width, index, tokens, gains, rows, normed, own_gains):
    to_own_order(index, tokens, rows, count, width)
    to_own_order(index, gains, own_gains, count, width)
    value = rows[...].astype(F32)
    normed[...] = (value * row_scale(value) * own_gains[0:1, :]).astype(BF)


def row_call(kernel, name, index, ins, outs, waits=()):
    total = max(a.shape[0] for a in ins)
    chunk = min(128, total)

    def spec(a):
        if a.shape[0] == total:
            return (chunk, a.shape[1]), lambda i, index: (i, 0)
        return a.shape, lambda i, index: (0, 0)

    return call(
        kernel,
        name,
        [(a, *spec(a)) for a in ins],
        [(a.shape, a.dtype, *spec(a)) for a in outs],
        (total // chunk,),
        waits=waits,
        table=index,
    )


def like(array, dtype):
    return jax.ShapeDtypeStruct(array.shape, dtype)


def order_kernel(count, width, index, source, target):
    to_own_order(index, source, target, count, width)


def middle_kernel(index, rows, moved, gains, middle, normed):
    value = rows[...].astype(F32) + moved[...].astype(F32)
    middle[...] = value
    normed[...] = (value * row_scale(value) * gains[1:2, :]).astype(BF)


def norm_back(rows, gain, upstream):
    scale = row_scale(rows)
    inner = jnp.mean(upstream * gain * rows, axis=-1, keepdims=True)
    part = jnp.sum(upstream * rows * scale, axis=0, keepdims=True)
    return scale * gain * upstream - rows * scale * scale * scale * inner, part


def middle_back_kernel(index, near, mate, moved, middle, upstream, gains, grad, low, part):
    @pl.when(pl.program_id(0) == 0)
    def _():
        part[...] = jnp.zeros_like(part)

    total = near[...].astype(F32) + mate[...].astype(F32) + moved[...].astype(F32)
    back, gain_part = norm_back(middle[...], gains[1:2, :], total)
    value = upstream[...].astype(F32) + back
    grad[...] = value
    low[...] = value.astype(BF)
    part[...] += gain_part


def out_kernel(count, width, index, near, mate, moved, middle, target):
    total = near[...].astype(F32) + mate[...].astype(F32) + moved[...].astype(F32)
    value = (middle[...] + total).astype(BF)
    to_array_order(index, value, target, count, width)


def final_kernel(count, width, index, moved, rows, grad, gains, target):
    back, _ = norm_back(rows[...].astype(F32), gains[0:1, :], moved[...].astype(F32))
    to_array_order(index, grad[...] + back, target, count, width)


def gains_kernel(count, width, index, first, second, target):
    to_array_order(index, first, target.at[0:1, :], count, width)
    to_array_order(index, second, target.at[1:2, :], count, width)


def call(kernel, name, ins, outs, grid, scratch=(), waits=(), table=None, into=()):
    waits = (*into, *waits)

    def spec(shape, block, index):
        if block is None:
            zeros = (0,) * len(shape)
            return pl.BlockSpec(shape, lambda *at: zeros, pipeline_mode=pl.Buffered(1))
        return pl.BlockSpec(block, index)

    def out_spec(shape, block, index):
        if block is None:
            zeros = (0,) * len(shape)
            return pl.BlockSpec(shape, lambda *at: zeros)
        return pl.BlockSpec(block, index)

    first = 0 if table is None else 1
    count = len(ins)

    def run(*refs):
        kernel(*refs[: first + count], *refs[first + count + len(waits) :])

    return pl.pallas_call(
        run,
        grid_spec=pltpu.PrefetchScalarGridSpec(
            num_scalar_prefetch=first,
            grid=grid,
            in_specs=[spec(x.shape, b, m) for x, b, m in ins]
            + [pl.BlockSpec(memory_space=pl.ANY)] * len(waits),
            out_specs=[out_spec(sh, b, m) for sh, _, b, m in outs],
            scratch_shapes=list(scratch),
        ),
        out_shape=[jax.ShapeDtypeStruct(sh, dt) for sh, dt, _, _ in outs],
        input_output_aliases={first + count + i: i for i in range(len(into))},
        compiler_params=params(),
        cost_estimate=cost(),
        name=name,
    )(*(() if table is None else (table,)), *(x for x, _, _ in ins), *waits)


def put(target, at, value):
    target[:, at : at + value.shape[1]] = value
    return at + value.shape[1]


def fill(target, at, end):
    if end > at:
        target[:, at:end] = jnp.zeros((target.shape[0], end - at), target.dtype)
    return end


def pack_kernel(q, k, v, z, wo, gate, up, down, first, second, third, fourth):
    at = 0
    for part in (q[...], k[...], v[...].T):
        at = put(first, at, part)
    fill(first, at, first.shape[1])
    for left, right, target in ((z, wo, second), (up, down, third)):
        at = put(target, 0, left[...].T)
        at = fill(target, at, target.shape[1] // 2)
        at = put(target, at, right[...].T)
        fill(target, at, target.shape[1])
    at = put(fourth, 0, gate[...].T)
    fill(fourth, at, fourth.shape[1])


def pack(q, k, v, z, wo, gate, up, down):
    rows = q.shape[0]
    cols = lanes(q.shape[1] + k.shape[1] + v.shape[0])
    widths = [cols] + [2 * lanes(x.shape[0]) for x in (z, up)] + [lanes(gate.shape[0])]
    return call(
        pack_kernel,
        "pack",
        [(x, None, None) for x in (q, k, v, z, wo, gate, up, down)],
        [((rows, w), BF, None, None) for w in widths],
        (1,),
    )


def join(pieces, cols=slice(None)):
    return jnp.concatenate([p[:, cols] for p in pieces], axis=0)


def project_kernel(count, tiles, normed, *refs):
    first, second, qkv, z = refs[:count], refs[count : 2 * count], refs[-2], refs[-1]
    at = pl.program_id(0)

    @pl.when(at < tiles)
    def _():
        qkv[...] = dot_nn(normed[...], join(first)).astype(BF)

    @pl.when(at >= tiles)
    def _():
        z[...] = dot_nn(normed[...], join(second))


def project(normed, first, second, cols, val_cols, waits):
    total = normed.shape[0]
    width = first[0].shape[0]
    tile = 256
    tiles, more = pl.cdiv(cols, tile), pl.cdiv(val_cols, tile)
    in_first = lambda i: (0, jnp.minimum(i, tiles - 1))
    in_second = lambda i: (0, jnp.maximum(i - tiles, 0))
    return call(
        partial(project_kernel, len(first), tiles),
        "project",
        [(normed, None, None)]
        + [(p, (width, tile), in_first) for p in first]
        + [(p, (width, tile), in_second) for p in second],
        [
            ((total, cols), BF, (total, tile), in_first),
            ((total, val_cols), F32, (total, tile), in_second),
        ],
        (tiles + more,),
        waits=waits,
    )


def right_part(pieces, cols):
    block = (pieces[0].shape[0], round_up(cols, 128))
    return [(p, block, lambda *i: (0, 1)) for p in pieces]


def left_part(pieces, cols):
    block = (pieces[0].shape[0], min(round_up(cols, 128), pieces[0].shape[1]))
    return [(p, block, lambda *i: (0, 0)) for p in pieces]


def normed_grad_kernel(width, groups, normed, gains, *refs):
    target, part = refs[-2], refs[-1]

    @pl.when(pl.program_id(0) == 0)
    def _():
        part[...] = jnp.zeros_like(part)

    def keep(j, total):
        cols = slice(j * width, (j + 1) * width)
        value = jnp.sum(total * normed[:, cols].astype(F32), axis=0, keepdims=True)
        part[:, cols] += value / gains[0:1, cols]

    spread_kernel(width, groups, *refs[:-1], keep=keep)


def spread_kernel(width, groups, *refs, keep=None):
    values, at = [], 0
    for lefts, _ in groups:
        values.append(jnp.concatenate([r[...] for r in refs[at : at + lefts]], axis=1))
        at += lefts
    target = refs[-1]
    for j in range(groups[0][1]):
        total = None
        for i, (value, (_, count)) in enumerate(zip(values, groups)):
            part = dot_nt(value, refs[at + i * count + j][:, : value.shape[1]])
            total = part if total is None else total + part
        target[:, j * width : (j + 1) * width] = total.astype(target.dtype)
        if keep is not None:
            keep(j, total)


def normed_grad(normed, gains, pairs, waits=()):
    total, features = normed.shape
    count = len(pairs[0][1])
    width = pairs[0][1][0][1][0]
    block = min(512, total)
    by_rows = lambda i: (i, 0)
    return call(
        partial(normed_grad_kernel, width, [(len(lefts), count) for lefts, _ in pairs]),
        "normed_grad",
        [(normed, (block, features), by_rows), (gains, None, None)]
        + [(x, (block, x.shape[1]), by_rows) for lefts, _ in pairs for x in lefts]
        + [spec for _, specs in pairs for spec in specs],
        [
            ((total, features), BF, (block, features), by_rows),
            ((1, features), F32, None, None),
        ],
        (total // block,),
        waits=waits,
    )


def spread(name, pairs, waits=()):
    total = pairs[0][0][0].shape[0]
    count = len(pairs[0][1])
    width = pairs[0][1][0][1][0]
    block = min(512, total)
    return call(
        partial(spread_kernel, width, [(len(lefts), count) for lefts, _ in pairs]),
        name,
        [(x, (block, x.shape[1]), lambda i: (i, 0)) for lefts, _ in pairs for x in lefts]
        + [spec for _, specs in pairs for spec in specs],
        [((total, width * count), BF, (block, width * count), lambda i: (i, 0))],
        (total // block,),
        waits=waits,
    )[0]


def spread_rows_kernel(width, groups, *refs):
    own, mate = refs[-2], refs[-1]
    count = groups[0][1]
    lefts, sets = refs[: len(groups)], refs[len(groups) : -2]
    values = [left[...] for left in lefts]
    rows = own.shape[0]
    for j in range(count):
        total = None
        for i, (cols, _) in enumerate(groups):
            part = dot_nt(values[i], sets[i * count + j][:, :cols])
            total = part if total is None else total + part
        total = total.astype(BF)
        turned = (j + count // 2) % count
        own[:, j * width : (j + 1) * width] = total[:rows]
        mate[:, turned * width : (turned + 1) * width] = total[rows:]


def spread_rows(name, pairs, place, waits=()):
    total = pairs[0][0].shape[0] // 2
    count = len(pairs[0][1])
    width = pairs[0][1][0][1][0]
    shape = (total // 2, width * count)
    return call(
        partial(spread_rows_kernel, width, [(x.shape[1], count) for x, _ in pairs]),
        name,
        [(x, (total, x.shape[1]), lambda i: (place, 0)) for x, _ in pairs]
        + [spec for _, specs in pairs for spec in specs],
        [(shape, BF, None, None)] * 2,
        (1,),
        waits=waits,
    )


def hidden_kernel(cols, steps, own, mate, *refs):
    pieces, target = refs[:-1], refs[-1]
    at = pl.program_id(0)
    half = len(pieces) // 2

    @pl.when(at < steps)
    def _():
        target[...] = dot_nn(own[...], join(pieces, slice(0, cols)))

    @pl.when(at >= steps)
    def _():
        turned = pieces[half:] + pieces[:half]
        target[...] = dot_nn(mate[...], join(turned, slice(0, cols)))


def hidden_side(own, mate, pieces, cols, waits=()):
    rows, features = own.shape
    block = min(256, rows)
    steps = rows // block
    return call(
        partial(hidden_kernel, lanes(cols), steps),
        "hidden_side",
        [
            (own, (block, features), lambda i: (jnp.minimum(i, steps - 1), 0)),
            (mate, (block, features), lambda i: (jnp.maximum(i - steps, 0), 0)),
        ]
        + right_part(pieces, cols),
        [((2 * rows, lanes(cols)), F32, (block, lanes(cols)), lambda i: (i, 0))],
        (2 * steps,),
        waits=waits,
    )[0]


def units_kernel(count, own, mate, grad, *refs):
    gates, ups = refs[:count], refs[count : 2 * count]
    hidden, gate_grad, up_grad = refs[2 * count :]
    rows = own.shape[0]
    half = count // 2
    for source, turn, place in ((own, 0, slice(0, rows)), (mate, half, slice(rows, 2 * rows))):
        value = source[...]
        a = dot_nn(value, join(gates[turn:] + gates[:turn]))
        b = dot_nn(value, join(ups[turn:] + ups[:turn]))
        inner = 0.7978845608028654 * (a + 0.044715 * (a * a * a))
        tanh = jnp.tanh(inner)
        cdf = 0.5 * (1.0 + tanh)
        gelu = a * cdf
        slope = cdf + 0.5 * a * (1.0 - tanh * tanh) * 0.7978845608028654 * (
            1.0 + 3.0 * 0.044715 * (a * a)
        )
        dh = grad[place, :]
        hidden[place, :] = (gelu * b).astype(BF)
        gate_grad[place, :] = (dh * b * slope).astype(BF)
        up_grad[place, :] = (dh * gelu).astype(BF)


def unit_rows(own, mate, gates, ups, grad, place, into=(), waits=()):
    rows, features = own.shape
    units = grad.shape[1]
    width = gates[0].shape[0]
    tile = min(256, units)
    by_tile = lambda j: (0, j)
    return call(
        partial(units_kernel, len(gates)),
        "unit_rows",
        [(own, None, None), (mate, None, None), (grad, (2 * rows, tile), by_tile)]
        + [(p, (width, tile), by_tile) for p in (*gates, *ups)],
        [((4 * rows, units), BF, (2 * rows, tile), lambda j: (place, j))] * 3,
        (pl.cdiv(units, tile),),
        waits=waits,
        into=into,
    )


def join_kernel(order, own, mate, pair, both, target):
    count = len(order)
    width = own.shape[1] // count
    rows = own.shape[0]
    for i, part in enumerate((own, mate, pair, both)):
        for at, number in enumerate(order):
            place = (number + count // 2) % count if i % 2 else number
            target[i * rows : (i + 1) * rows, at * width : (at + 1) * width] = part[
                :, place * width : (place + 1) * width
            ]


def block_order(bits):
    count = lax.axis_size("wide")
    return sorted(range(count), key=lambda j: tuple(j >> b & 1 for b in bits) + (j,))


def join_rows(parts, bits, waits=()):
    rows, features = parts[0].shape
    return call(
        partial(join_kernel, block_order(bits)),
        "join_rows",
        [(x, None, None) for x in parts],
        [((4 * rows, features), BF, None, None)],
        (1,),
        waits=waits,
    )[0]


def row_major(array):
    return with_layout_constraint(array, Layout(tuple(range(array.ndim))))


def weight_grads(left, right):
    count = lax.axis_size("wide")
    half = left.shape[1] // 2

    def part(columns):
        value = jnp.einsum("na,nb->ab", columns, right, preferred_element_type=F32).astype(BF)
        return row_major(value.reshape(count // 2, -1, right.shape[1]))

    return part(left[:, half:]), part(left[:, :half])


def branch_kernel(heads, cols, rows, z, mixed, *refs):
    pieces, dz, down = refs[:-2], refs[-2], refs[-1]
    dy = dot_nn(rows[...], join(pieces, slice(0, cols)))
    for h in range(heads):
        at = slice(h * VAL, (h + 1) * VAL)
        grouped, inverse = normalize(mixed[h])
        gate, upstream = z[:, at], dy[:, at]
        sig = jax.nn.sigmoid(gate)
        dz[:, at] = (upstream * grouped * (sig + gate * sig * (1.0 - sig))).astype(BF)
        dg = upstream * (gate * sig)
        first = jnp.mean(dg, axis=-1, keepdims=True)
        second = jnp.mean(dg * grouped, axis=-1, keepdims=True)
        down[h] = (inverse * (dg - first - grouped * second)).astype(BF)
    fill(dz, cols, dz.shape[1])


def branch_back(rows, z, mixed, pieces, waits=()):
    heads, total, _ = mixed.shape
    cols = heads * VAL
    block = min(256, total)
    by_rows = lambda i: (i, 0)
    by_heads = lambda i: (0, i, 0)
    return call(
        partial(branch_kernel, heads, cols),
        "branch_back",
        [
            (rows, (block, rows.shape[1]), by_rows),
            (z, (block, cols), by_rows),
            (mixed, (heads, block, VAL), by_heads),
        ]
        + right_part(pieces, cols),
        [
            ((total, lanes(cols)), BF, (block, lanes(cols)), by_rows),
            ((heads, total, VAL), BF, (heads, block, VAL), by_heads),
        ],
        (total // block,),
        waits=waits,
    )


def weight_block(rate, row_seg, col_seg, offset, block):
    down = lax.broadcasted_iota(jnp.int32, (block, block), 0)
    across = lax.broadcasted_iota(jnp.int32, (block, block), 1)
    gap = offset + down - across
    allowed = (gap >= 0) & (row_seg == col_seg)
    return jnp.where(allowed, jnp.exp(-rate * jnp.maximum(gap, 0).astype(F32)), 0.0)


def normalize(mixed):
    centred = mixed - jnp.mean(mixed, axis=-1, keepdims=True)
    inverse = lax.rsqrt(jnp.mean(centred * centred, axis=-1, keepdims=True) + 1.0)
    return centred * inverse, inverse


def forward_kernel(block, steps, heads, rate, seg_col, seg_row, qkv, z, gated, mixed, values, acc):
    at = pl.program_id(0)
    rows = pl.ds(pl.multiple_of(at * block, block), block)
    key_at, val_at = heads * KEY, 2 * heads * KEY

    @pl.when(at == 0)
    def _():
        for h in range(heads):
            values[h] = qkv[:, val_at + h * VAL : val_at + (h + 1) * VAL]

    acc[...] = jnp.zeros_like(acc)
    for step in range(steps):

        @pl.when(step <= at)
        def _():
            cols = pl.ds(step * block, block)
            for h in range(heads):
                weight = weight_block(
                    rate[0:1, h : h + 1], seg_col[...], seg_row[:, cols], (at - step) * block, block
                )
                q = qkv[rows, h * KEY : (h + 1) * KEY]
                k = qkv[cols, key_at + h * KEY : key_at + (h + 1) * KEY]
                probs = (dot_nt(q, k) * weight).astype(BF)
                acc[h] += dot_nn(probs, values[h, cols, :])

    for h in range(heads):
        total = acc[h]
        grouped, _ = normalize(total)
        mixed[h] = total
        gate = z[:, h * VAL : (h + 1) * VAL]
        gated[:, h * VAL : (h + 1) * VAL] = (gate * jax.nn.sigmoid(gate) * grouped).astype(BF)
    fill(gated, heads * VAL, gated.shape[1])


def retain_forward(qkv, z, seg_row, seg_col, rate, waits=()):
    total = qkv.shape[0]
    heads = rate.shape[1]
    block = min(256, total)
    steps = total // block
    by_rows = lambda i: (i, 0)
    by_heads = lambda i: (0, i, 0)
    return call(
        partial(forward_kernel, block, steps, heads),
        "retain_forward",
        [
            (rate, None, None),
            (seg_col, (block, 1), by_rows),
            (seg_row, None, None),
            (qkv, None, None),
            (z, (block, heads * VAL), by_rows),
        ],
        [
            ((total, lanes(heads * VAL)), BF, (block, lanes(heads * VAL)), by_rows),
            ((heads, total, VAL), F32, (heads, block, VAL), by_heads),
        ],
        (steps,),
        [pltpu.VMEM((heads, total, VAL), BF), pltpu.VMEM((heads, block, VAL), F32)],
        waits,
    )


def backward_kernel(
    block, steps, heads, rate, seg_col, seg_row, qkv, down, grads, val_grads, values, dk_acc, dv_acc, dq_acc
):
    at = pl.program_id(0)
    rows = pl.ds(pl.multiple_of(at * block, block), block)
    key_at, val_at = heads * KEY, 2 * heads * KEY

    @pl.when(at == 0)
    def _():
        dk_acc[...] = jnp.zeros_like(dk_acc)
        dv_acc[...] = jnp.zeros_like(dv_acc)
        for h in range(heads):
            values[h] = qkv[:, val_at + h * VAL : val_at + (h + 1) * VAL]

    dq_acc[...] = jnp.zeros_like(dq_acc)
    for step in range(steps):

        @pl.when(step <= at)
        def _():
            cols = pl.ds(step * block, block)
            for h in range(heads):
                weight = weight_block(
                    rate[0:1, h : h + 1], seg_col[...], seg_row[:, cols], (at - step) * block, block
                )
                q = qkv[rows, h * KEY : (h + 1) * KEY]
                k = qkv[cols, key_at + h * KEY : key_at + (h + 1) * KEY]
                probs = (dot_nt(q, k) * weight).astype(BF)
                score_grad = (dot_nt(down[h], values[h, cols, :]) * weight).astype(BF)
                dq_acc[h] += dot_nn(score_grad, k)
                dk_acc[h, cols, :] += dot_tn(score_grad, q)
                dv_acc[h, cols, :] += dot_tn(probs, down[h])

    for h in range(heads):
        grads[rows, h * KEY : (h + 1) * KEY] = dq_acc[h].astype(BF)

    @pl.when(at == steps - 1)
    def _():
        for h in range(heads):
            grads[:, key_at + h * KEY : key_at + (h + 1) * KEY] = dk_acc[h].astype(BF)
            val_grads[:, h * VAL : (h + 1) * VAL] = dv_acc[h].astype(BF)
        fill(val_grads, heads * VAL, val_grads.shape[1])


def retain_backward(qkv, down, seg_row, seg_col, rate, waits=()):
    total = qkv.shape[0]
    heads = rate.shape[1]
    block = min(256, total)
    steps = total // block
    return call(
        partial(backward_kernel, block, steps, heads),
        "retain_backward",
        [
            (rate, None, None),
            (seg_col, (block, 1), lambda i: (i, 0)),
            (seg_row, None, None),
            (qkv, None, None),
            (down, (heads, block, VAL), lambda i: (0, i, 0)),
        ],
        [((total, 2 * heads * KEY), BF, None, None), ((total, lanes(heads * VAL)), BF, None, None)],
        (steps,),
        [
            pltpu.VMEM((heads, total, VAL), BF),
            pltpu.VMEM((heads, total, KEY), F32),
            pltpu.VMEM((heads, total, VAL), F32),
            pltpu.VMEM((heads, block, KEY), F32),
        ],
        waits,
    )


def swap_wide(array, mask):
    count = lax.axis_size("wide")
    return lax.ppermute(array, "wide", [(i, i ^ mask) for i in range(count)])


def swap_tensor(array, mask):
    count = lax.axis_size("tensor")
    return lax.ppermute(array, "tensor", [(i, i ^ mask) for i in range(count)])


def top_bit():
    return lax.axis_size("wide").bit_length() - 2


def mask_of(bit):
    return 1 if bit == top_bit() else 2 << bit


def double(first, second, bits, cores, sync, late=()):
    top = 1 << top_bit()
    mates_first, mates_second = {}, {}
    new = (0, 0)

    def to_mates(sync):
        mates_first[new[0] | top] = swap_wide(first[new[0]], 1)
        mates_second[new[1] | top] = swap_wide(second[new[1]], 1)
        return (mates_first[new[0] | top], mates_second[new[1] | top])

    for place, (bit_first, bit_second) in enumerate(bits):
        count = len(first)
        for step, (one, two) in enumerate(zip(list(first), list(second))):
            if place == len(bits) - 1 and step == count - 1:
                sync = (*sync, *late)
            sent = after((first[one], second[two]), *sync) if sync else (first[one], second[two])
            sync = to_mates(sync) if cores else ()
            new = (one | 1 << bit_first, two | 1 << bit_second)
            first[new[0]] = swap_wide(sent[0], mask_of(bit_first))
            second[new[1]] = swap_wide(sent[1], mask_of(bit_second))
            sync = (first[new[0]], second[new[1]], *sync)
    if cores:
        sync = to_mates(sync)
        first.update(mates_first)
        second.update(mates_second)
    return sync


def listed(pieces):
    return [pieces[number] for number in range(len(pieces))]


def far_pairs():
    count = lax.axis_size("tensor")
    return [[i, i ^ 2] for i in range(count) if not i & 2]


def choose(straight, left, right):
    return jnp.where(straight, left, right), jnp.where(straight, right, left)


def exchange_units(block, got, even):
    own, given = choose(even, block, got)
    return {0: own}, {0: swap_wide(given, 1)}


def widen_units(pieces, cols, parts):
    mask = 4
    while mask < lax.axis_size("tensor"):
        pieces = {n: beside(p, swap_tensor(p, mask), cols, parts) for n, p in pieces.items()}
        cols *= 2
        mask *= 2
    return pieces


def beside(left, right, cols, parts):
    step = round_up(cols, 128)
    rest = jnp.zeros((left.shape[0], round_up(2 * cols, 128) - 2 * cols), left.dtype)
    out = []
    for i in range(parts):
        at = slice(i * step, i * step + cols)
        out += [left[:, at], right[:, at], rest]
    return jnp.concatenate(out, axis=1)


def fold(kept, got, low=False):
    half = kept.shape[0] // 2
    places = (slice(1, None, 2), slice(0, None, 2)) if low else (slice(half, None), slice(0, half))
    away, stay = (
        row_major((kept[p].astype(F32) + got[p].astype(F32)).astype(BF)) for p in places
    )
    return away, stay


def reduce_step(away, kept, bit, low=False):
    return fold(kept, swap_wide(away, mask_of(bit)), low)


def reduce_last(away, kept, bit, waits):
    got = swap_wide(away, mask_of(bit))[0]
    return kept[0].astype(F32) + after(got, *waits).astype(F32)


def reduce_chip(away, kept, bits, waits):
    for place, bit in enumerate(bits):
        got = swap_wide(away, mask_of(bit))
        if place in waits:
            got = after(got, *waits[place])
        away, kept = fold(kept, got)
    return kept[0], away[0]


def reduce_units(own, mate, cols, straight):
    mask = lax.axis_size("tensor") // 2
    while mask >= 4:
        cols //= 2
        own, mate = (
            (
                p[:, :cols].astype(F32) + swap_tensor(p[:, cols : 2 * cols], mask).astype(F32)
            ).astype(BF)
            for p in (own, mate)
        )
        mask //= 2
    return jnp.stack(choose(straight, own, swap_wide(mate, 1)))


def add_pair(pair):
    return pair[0].astype(F32) + pair[1].astype(F32)


def after(value, *earlier):
    return lax.optimization_barrier((value, earlier))[0]


def sum_all(array):
    mask = 1
    while mask < lax.axis_size("tensor"):
        array = array + swap_tensor(array, mask)
        mask *= 2
    mask = 1
    while mask < lax.axis_size("wide"):
        array = array + swap_wide(array, mask)
        mask *= 2
    return array


def body(
    tokens,
    query_weight,
    key_weight,
    value_weight,
    swish_weight,
    output_weight,
    mlp_gate,
    mlp_up,
    mlp_down,
    gain_one,
    gain_two,
    segments,
    decay_rate,
    cotangent,
):
    wide = lax.axis_size("wide")
    me = lax.axis_index("wide")
    top = top_bit()
    chip_bits = list(range(top))
    turned = chip_bits[::-1]
    numbers = jnp.arange(wide, dtype=jnp.int32)
    index = me ^ (((numbers << 1) & (wide - 1)) | (numbers >> top))
    features = tokens.shape[1]
    width = features // wide

    heads = query_weight.shape[1] // KEY
    key_cols = heads * KEY
    val_cols = heads * VAL
    own_units = mlp_gate.shape[1]
    val_pad = lanes(val_cols)
    rate = decay_rate.reshape(1, heads)

    rows, normed_local, gains = row_call(
        partial(entry_kernel, wide, width),
        "entry",
        index,
        [tokens, jnp.stack([gain_one, gain_two])],
        [like(tokens, BF), like(tokens, BF), jax.ShapeDtypeStruct((2, features), F32)],
    )
    normed = lax.all_gather(normed_local, "tensor", axis=0, tiled=True)
    total = normed.shape[0]

    block_a, block_b, block_u, block_g = pack(
        query_weight,
        key_weight,
        value_weight.T,
        swish_weight.T,
        output_weight,
        mlp_gate.T,
        mlp_up.T,
        mlp_down,
    )
    even = (me & 1) == 0
    straight = ((me ^ lax.axis_index("tensor") >> 1) & 1) == 0
    (upstream,) = row_call(
        partial(order_kernel, wide, width), "order", index, [cotangent], [like(cotangent, BF)]
    )
    crossing, opposite = list(zip(chip_bits, turned)), list(zip(turned, chip_bits))
    pieces_a, pieces_b = {0: block_a}, {0: block_b}
    double(pieces_a, pieces_b, crossing, True, (), (upstream,))
    pieces_a, pieces_b = listed(pieces_a), listed(pieces_b)

    qkv_cols = 2 * key_cols + val_cols
    gate_sent, up_sent, upstream_sent = after((block_g, block_u, upstream), normed)
    qkv, z = project(normed, pieces_a, pieces_b, qkv_cols, val_cols, (upstream,))
    gate_got, up_got = swap_tensor(gate_sent, 2), swap_tensor(up_sent, 2)
    upstream_pair = swap_tensor(upstream_sent, 1)
    gates_own, gates_mate = exchange_units(block_g, after(gate_got, qkv), even)
    units = own_units * lax.axis_size("tensor") // 4
    gates_own, gates_mate = (widen_units(p, own_units, 1) for p in (gates_own, gates_mate))
    double(gates_own, gates_mate, crossing[:1], False, ())
    seg_row = segments
    seg_col = segments.reshape(total, 1)
    gated, mixed = retain_forward(
        qkv, z, seg_row, seg_col, rate
    )
    early = (gates_own[1], gates_mate[1 << turned[0]])
    sync = double(gates_own, gates_mate, crossing[1:], False, (gated,))
    gates = listed({**gates_own, **{n | 1 << top: p for n, p in gates_mate.items()}})
    projected = spread(
        "project_out",
        [((gated,), right_part(pieces_b, val_pad))],
        (up_got, upstream_pair, *early),
    )
    moved_up = lax.psum_scatter(projected, "tensor", scatter_dimension=0, tiled=True)

    ups_own, ups_mate = exchange_units(block_u, up_got, even)
    ups_own, ups_mate = (widen_units(p, own_units, 2) for p in (ups_own, ups_mate))
    double(ups_own, ups_mate, opposite, False, ())
    ups = listed({**ups_own, **{n | 1 << top: p for n, p in ups_mate.items()}})
    upstream_mate = swap_wide(upstream, 1)
    upstream_both = swap_wide(upstream_pair, 1)
    down_rows = join_rows(
        (upstream, upstream_mate, upstream_pair, upstream_both), chip_bits, (projected,)
    )
    near_hidden = hidden_side(upstream, upstream_mate, ups, units, (down_rows,))
    middle, normed_two_local = row_call(
        middle_kernel,
        "middle",
        index,
        [rows, moved_up, gains],
        [like(rows, F32), like(rows, BF)],
        (near_hidden, *gates),
    )

    own = normed_two_local
    pair = swap_tensor(own, 1)
    mate = swap_wide(own, 1)
    near = unit_rows(own, mate, gates, ups, near_hidden, 0)
    unit_pad = lanes(units)

    def input_side(parts, place, waits=()):
        return spread_rows(
            "input_side",
            [(parts[1], left_part(gates, unit_pad)), (parts[2], left_part(ups, unit_pad))],
            place,
            waits,
        )

    def output_side(parts, place, waits=()):
        return spread_rows("output_side", [(parts[0], right_part(ups, unit_pad))], place, waits)

    far_hidden = hidden_side(upstream_pair, upstream_both, ups, units, (near[0],))
    pair = after(pair, far_hidden)
    both = swap_wide(pair, 1)
    hidden, gate_rows, up_rows = unit_rows(pair, both, gates, ups, far_hidden, 1, near)
    unit_parts = (hidden, gate_rows, up_rows)
    far_own, far_mate = input_side(unit_parts, 1)
    far_sent = (far_own.astype(F32) + swap_wide(far_mate, 1).astype(F32)).astype(BF)
    moved_far = swap_tensor(far_sent, 1)
    near_own, near_mate = input_side(unit_parts, 0, (far_sent,))
    near_got = swap_wide(near_mate, 1)
    unit_tokens = join_rows((own, mate, pair, both), turned, (near_own,))
    gate_away, gate_kept = weight_grads(unit_tokens, gate_rows)
    down_left = after(down_rows, gate_away)
    down_away, down_kept = weight_grads(down_left, hidden)
    middle_grad, branch_local, gain_two_part = row_call(
        middle_back_kernel,
        "middle_back",
        index,
        [near_own, near_got, moved_far, middle, upstream, gains],
        [like(rows, F32), like(rows, BF), jax.ShapeDtypeStruct((1, features), F32)],
        (down_away,),
    )
    branch_rows = lax.all_gather(branch_local, "tensor", axis=0, tiled=True)

    up_left = after(unit_tokens, branch_local)
    up_away, up_kept = weight_grads(up_left, up_rows)
    out_far_own, out_far_mate = output_side(unit_parts, 1, (up_away,))
    out_near_own, out_near_mate = output_side(unit_parts, 0, (out_far_own,))
    out_sent = (out_far_own.astype(F32) + swap_wide(out_far_mate, 1).astype(F32)).astype(BF)
    out_got = swap_wide(out_near_mate, 1)
    outs = {0: (out_near_own,)}
    gate_part = reduce_chip(gate_away, gate_kept, turned, outs)

    gate_far = reduce_units(*gate_part, units, straight)
    swish_rows, down = branch_back(branch_rows, z, mixed, pieces_b, (out_sent, gate_far))
    late = {**outs, top - 1: (swish_rows,)}
    down_part = reduce_chip(down_away, down_kept, chip_bits, late)
    up_part = reduce_chip(up_away, up_kept, turned, {n: (swish_rows,) for n in range(top)})

    def far(part):
        return reduce_units(*part, units, straight)

    def sum_far(array):
        return lax.psum_scatter(array, "tensor", axis_index_groups=pairs)

    pairs = far_pairs()
    gate_sum = sum_far(after(gate_far, branch_rows))
    down_up_far = jnp.concatenate([far(down_part), far(up_part)], axis=1)
    down_up_sum = sum_far(after(down_up_far, gate_sum))
    out_moved = swap_tensor(after(out_sent, branch_rows), 1)
    qk_rows, v_rows = retain_backward(qkv, down, seg_row, seg_col, rate, (down_up_far, gate_sum))

    order_a, order_b = [top] + turned, [top] + chip_bits
    qk_parts = weight_grads(normed, qk_rows)
    v_parts = weight_grads(after(normed, qk_parts[1]), v_rows)
    swish_parts = weight_grads(after(normed, v_parts[1]), swish_rows)
    out_parts = weight_grads(after(branch_rows, swish_parts[1]), gated)
    qk_parts = reduce_step(*qk_parts, top)
    v_parts = reduce_step(*v_parts, top, True)
    total_term, gain_one_part = normed_grad(
        normed,
        gains,
        [
            ((qk_rows, v_rows), left_part(pieces_a, 2 * key_cols + val_pad)),
            ((swish_rows,), left_part(pieces_b, val_pad)),
        ],
        (*out_parts, qk_parts[0], v_parts[0]),
    )
    total_term = after(total_term, down_up_sum, out_moved)
    moved_down = lax.psum_scatter(total_term, "tensor", scatter_dimension=0, tiled=True)
    swish_parts = reduce_step(*swish_parts, top, True)
    out_parts = reduce_step(*out_parts, top)
    for bit in order_b[1:-1]:
        swish_parts = reduce_step(*swish_parts, bit, True)
    for bit in order_a[1:-1]:
        out_parts = reduce_step(*out_parts, bit)
    (layer_out,) = row_call(
        partial(out_kernel, wide, width),
        "layer_out",
        index,
        [out_near_own, out_got, out_moved, middle],
        [like(rows, BF)],
        (v_parts[0],),
    )
    for bit in order_a[1:-1]:
        qk_parts = reduce_step(*qk_parts, bit)
    for bit in order_b[1:-1]:
        v_parts = reduce_step(*v_parts, bit, True)
    (gain_parts,) = call(
        partial(gains_kernel, wide, width),
        "gains",
        [(gain_one_part, None, None), (gain_two_part, None, None)],
        [((2, features), F32, None, None)],
        (1,),
        table=index,
    )
    gain_sums = sum_all(gain_parts)
    (input_grad,) = row_call(
        partial(final_kernel, wide, width),
        "final",
        index,
        [moved_down, rows, middle_grad, gains],
        [like(rows, F32)],
        (layer_out, gain_sums),
    )
    late = (input_grad,)
    swish_sum, v_sum = (reduce_last(*p, order_b[-1], late) for p in (swish_parts, v_parts))
    output_sum, qk_sum = (reduce_last(*p, order_a[-1], late) for p in (out_parts, qk_parts))
    weight_sums = (
        qk_sum[:, :key_cols],
        qk_sum[:, key_cols:],
        v_sum[:, :val_cols],
        swish_sum[:, :val_cols],
        output_sum[:, :val_cols].T,
        gate_sum[:, :own_units].astype(F32),
        down_up_sum[width:, :own_units].astype(F32),
        down_up_sum[:width, :own_units].astype(F32).T,
    )
    return (layer_out, input_grad, *weight_sums, gain_sums[0], gain_sums[1])


def solution(mesh):
    tokens_at = P(("wide", "tensor"), None)
    by_rows = P("wide", "tensor")
    by_cols = P("tensor", "wide")
    in_specs = (
        tokens_at,
        by_rows,
        by_rows,
        by_rows,
        by_rows,
        by_cols,
        by_rows,
        by_rows,
        by_cols,
        P(),
        P(),
        P("wide", None),
        P("tensor"),
        tokens_at,
    )
    out_specs = (
        tokens_at,
        tokens_at,
        by_rows,
        by_rows,
        by_rows,
        by_rows,
        by_cols,
        by_rows,
        by_rows,
        by_cols,
        P(),
        P(),
    )
    return jax.shard_map(body, mesh=mesh, in_specs=in_specs, out_specs=out_specs, check_vma=False)
```

```python
from functools import partial

import jax
import jax.numpy as jnp
from jax import lax
from jax.experimental import pallas as pl
from jax.experimental.layout import Layout, with_layout_constraint
from jax.experimental.pallas import tpu as pltpu
from jax.sharding import PartitionSpec as P

KEY = 256
VAL = 432
BF = jnp.bfloat16
F32 = jnp.float32
VMEM_LIMIT = 56 * 1024 * 1024


def round_up(count, step):
    return -(-count // step) * step


def lanes(count):
    return round_up(count, 128)


def dot_nt(left, right):
    return lax.dot_general(left, right, (((1,), (1,)), ((), ())), preferred_element_type=F32)


def dot_tn(left, right):
    return lax.dot_general(left, right, (((0,), (0,)), ((), ())), preferred_element_type=F32)


def dot_nn(left, right):
    return lax.dot_general(left, right, (((1,), (0,)), ((), ())), preferred_element_type=F32)


def params():
    return pltpu.CompilerParams(vmem_limit_bytes=VMEM_LIMIT)


def cost():
    return pl.CostEstimate(flops=1000000, transcendentals=0, bytes_accessed=0)


def row_scale(rows):
    return lax.rsqrt(jnp.mean(rows * rows, axis=-1, keepdims=True) + 1e-06)


def to_own_order(index, source, target, count, width):
    for j in range(count):
        place = pl.ds(pl.multiple_of(index[j] * width, width), width)
        target[:, j * width : (j + 1) * width] = source[:, place]


def to_array_order(index, value, target, count, width):
    for j in range(count):
        place = pl.ds(pl.multiple_of(index[j] * width, width), width)
        target[:, place] = value[:, j * width : (j + 1) * width]


def entry_kernel(count, width, index, tokens, gains, rows, normed, own_gains):
    to_own_order(index, tokens, rows, count, width)
    to_own_order(index, gains, own_gains, count, width)
    value = rows[...].astype(F32)
    normed[...] = (value * row_scale(value) * own_gains[0:1, :]).astype(BF)


def row_call(kernel, name, index, ins, outs, waits=()):
    total = max(a.shape[0] for a in ins)
    chunk = min(128, total)

    def spec(a):
        if a.shape[0] == total:
            return (chunk, a.shape[1]), lambda i, index: (i, 0)
        return a.shape, lambda i, index: (0, 0)

    return call(
        kernel,
        name,
        [(a, *spec(a)) for a in ins],
        [(a.shape, a.dtype, *spec(a)) for a in outs],
        (total // chunk,),
        waits=waits,
        table=index,
    )


def like(array, dtype):
    return jax.ShapeDtypeStruct(array.shape, dtype)


def order_kernel(count, width, index, source, target):
    to_own_order(index, source, target, count, width)


def middle_kernel(index, rows, moved, gains, middle, normed):
    value = rows[...].astype(F32) + moved[...].astype(F32)
    middle[...] = value
    normed[...] = (value * row_scale(value) * gains[1:2, :]).astype(BF)


def norm_back(rows, gain, upstream):
    scale = row_scale(rows)
    inner = jnp.mean(upstream * gain * rows, axis=-1, keepdims=True)
    part = jnp.sum(upstream * rows * scale, axis=0, keepdims=True)
    return scale * gain * upstream - rows * scale * scale * scale * inner, part


def middle_back_kernel(index, near, mate, moved, middle, upstream, gains, grad, low, part):
    @pl.when(pl.program_id(0) == 0)
    def _():
        part[...] = jnp.zeros_like(part)

    total = near[...].astype(F32) + mate[...].astype(F32) + moved[...].astype(F32)
    back, gain_part = norm_back(middle[...], gains[1:2, :], total)
    value = upstream[...].astype(F32) + back
    grad[...] = value
    low[...] = value.astype(BF)
    part[...] += gain_part


def out_kernel(count, width, index, near, mate, moved, middle, target):
    total = near[...].astype(F32) + mate[...].astype(F32) + moved[...].astype(F32)
    value = (middle[...] + total).astype(BF)
    to_array_order(index, value, target, count, width)


def final_kernel(count, width, index, moved, rows, grad, gains, target):
    back, _ = norm_back(rows[...].astype(F32), gains[0:1, :], moved[...].astype(F32))
    to_array_order(index, grad[...] + back, target, count, width)


def gains_kernel(count, width, index, first, second, target):
    to_array_order(index, first, target.at[0:1, :], count, width)
    to_array_order(index, second, target.at[1:2, :], count, width)


def call(kernel, name, ins, outs, grid, scratch=(), waits=(), table=None, into=()):
    waits = (*into, *waits)

    def spec(shape, block, index):
        if block is None:
            zeros = (0,) * len(shape)
            return pl.BlockSpec(shape, lambda *at: zeros, pipeline_mode=pl.Buffered(1))
        return pl.BlockSpec(block, index)

    def out_spec(shape, block, index):
        if block is None:
            zeros = (0,) * len(shape)
            return pl.BlockSpec(shape, lambda *at: zeros)
        return pl.BlockSpec(block, index)

    first = 0 if table is None else 1
    count = len(ins)

    def run(*refs):
        kernel(*refs[: first + count], *refs[first + count + len(waits) :])

    return pl.pallas_call(
        run,
        grid_spec=pltpu.PrefetchScalarGridSpec(
            num_scalar_prefetch=first,
            grid=grid,
            in_specs=[spec(x.shape, b, m) for x, b, m in ins]
            + [pl.BlockSpec(memory_space=pl.ANY)] * len(waits),
            out_specs=[out_spec(sh, b, m) for sh, _, b, m in outs],
            scratch_shapes=list(scratch),
        ),
        out_shape=[jax.ShapeDtypeStruct(sh, dt) for sh, dt, _, _ in outs],
        input_output_aliases={first + count + i: i for i in range(len(into))},
        compiler_params=params(),
        cost_estimate=cost(),
        name=name,
    )(*(() if table is None else (table,)), *(x for x, _, _ in ins), *waits)


def put(target, at, value):
    target[:, at : at + value.shape[1]] = value
    return at + value.shape[1]


def fill(target, at, end):
    if end > at:
        target[:, at:end] = jnp.zeros((target.shape[0], end - at), target.dtype)
    return end


def pack_kernel(q, k, v, z, wo, gate, up, down, first, second, third, fourth):
    at = 0
    for part in (q[...], k[...], v[...].T):
        at = put(first, at, part)
    fill(first, at, first.shape[1])
    for left, right, target in ((z, wo, second), (up, down, third)):
        at = put(target, 0, left[...].T)
        at = fill(target, at, target.shape[1] // 2)
        at = put(target, at, right[...].T)
        fill(target, at, target.shape[1])
    at = put(fourth, 0, gate[...].T)
    fill(fourth, at, fourth.shape[1])


def pack(q, k, v, z, wo, gate, up, down):
    rows = q.shape[0]
    cols = lanes(q.shape[1] + k.shape[1] + v.shape[0])
    widths = [cols] + [2 * lanes(x.shape[0]) for x in (z, up)] + [lanes(gate.shape[0])]
    return call(
        pack_kernel,
        "pack",
        [(x, None, None) for x in (q, k, v, z, wo, gate, up, down)],
        [((rows, w), BF, None, None) for w in widths],
        (1,),
    )


def join(pieces, cols=slice(None)):
    return jnp.concatenate([p[:, cols] for p in pieces], axis=0)


def project_kernel(count, tiles, normed, *refs):
    first, second, qkv, z = refs[:count], refs[count : 2 * count], refs[-2], refs[-1]
    at = pl.program_id(0)

    @pl.when(at < tiles)
    def _():
        qkv[...] = dot_nn(normed[...], join(first)).astype(BF)

    @pl.when(at >= tiles)
    def _():
        z[...] = dot_nn(normed[...], join(second))


def project(normed, first, second, cols, val_cols, waits):
    total = normed.shape[0]
    width = first[0].shape[0]
    tile = 256
    tiles, more = pl.cdiv(cols, tile), pl.cdiv(val_cols, tile)
    in_first = lambda i: (0, jnp.minimum(i, tiles - 1))
    in_second = lambda i: (0, jnp.maximum(i - tiles, 0))
    return call(
        partial(project_kernel, len(first), tiles),
        "project",
        [(normed, None, None)]
        + [(p, (width, tile), in_first) for p in first]
        + [(p, (width, tile), in_second) for p in second],
        [
            ((total, cols), BF, (total, tile), in_first),
            ((total, val_cols), F32, (total, tile), in_second),
        ],
        (tiles + more,),
        waits=waits,
    )


def right_part(pieces, cols):
    block = (pieces[0].shape[0], round_up(cols, 128))
    return [(p, block, lambda *i: (0, 1)) for p in pieces]


def left_part(pieces, cols):
    block = (pieces[0].shape[0], min(round_up(cols, 128), pieces[0].shape[1]))
    return [(p, block, lambda *i: (0, 0)) for p in pieces]


def normed_grad_kernel(width, groups, normed, gains, *refs):
    target, part = refs[-2], refs[-1]

    @pl.when(pl.program_id(0) == 0)
    def _():
        part[...] = jnp.zeros_like(part)

    def keep(j, total):
        cols = slice(j * width, (j + 1) * width)
        value = jnp.sum(total * normed[:, cols].astype(F32), axis=0, keepdims=True)
        part[:, cols] += value / gains[0:1, cols]

    spread_kernel(width, groups, *refs[:-1], keep=keep)


def spread_kernel(width, groups, *refs, keep=None):
    values, at = [], 0
    for lefts, _ in groups:
        values.append(jnp.concatenate([r[...] for r in refs[at : at + lefts]], axis=1))
        at += lefts
    target = refs[-1]
    for j in range(groups[0][1]):
        total = None
        for i, (value, (_, count)) in enumerate(zip(values, groups)):
            part = dot_nt(value, refs[at + i * count + j][:, : value.shape[1]])
            total = part if total is None else total + part
        target[:, j * width : (j + 1) * width] = total.astype(target.dtype)
        if keep is not None:
            keep(j, total)


def normed_grad(normed, gains, pairs, waits=()):
    total, features = normed.shape
    count = len(pairs[0][1])
    width = pairs[0][1][0][1][0]
    block = min(512, total)
    by_rows = lambda i: (i, 0)
    return call(
        partial(normed_grad_kernel, width, [(len(lefts), count) for lefts, _ in pairs]),
        "normed_grad",
        [(normed, (block, features), by_rows), (gains, None, None)]
        + [(x, (block, x.shape[1]), by_rows) for lefts, _ in pairs for x in lefts]
        + [spec for _, specs in pairs for spec in specs],
        [
            ((total, features), BF, (block, features), by_rows),
            ((1, features), F32, None, None),
        ],
        (total // block,),
        waits=waits,
    )


def spread(name, pairs, waits=()):
    total = pairs[0][0][0].shape[0]
    count = len(pairs[0][1])
    width = pairs[0][1][0][1][0]
    block = min(512, total)
    return call(
        partial(spread_kernel, width, [(len(lefts), count) for lefts, _ in pairs]),
        name,
        [(x, (block, x.shape[1]), lambda i: (i, 0)) for lefts, _ in pairs for x in lefts]
        + [spec for _, specs in pairs for spec in specs],
        [((total, width * count), BF, (block, width * count), lambda i: (i, 0))],
        (total // block,),
        waits=waits,
    )[0]


def spread_rows_kernel(width, groups, *refs):
    own, mate = refs[-2], refs[-1]
    count = groups[0][1]
    lefts, sets = refs[: len(groups)], refs[len(groups) : -2]
    values = [left[...] for left in lefts]
    rows = own.shape[0]
    for j in range(count):
        total = None
        for i, (cols, _) in enumerate(groups):
            part = dot_nt(values[i], sets[i * count + j][:, :cols])
            total = part if total is None else total + part
        total = total.astype(BF)
        turned = (j + count // 2) % count
        own[:, j * width : (j + 1) * width] = total[:rows]
        mate[:, turned * width : (turned + 1) * width] = total[rows:]


def spread_rows(name, pairs, place, waits=()):
    total = pairs[0][0].shape[0] // 2
    count = len(pairs[0][1])
    width = pairs[0][1][0][1][0]
    shape = (total // 2, width * count)
    return call(
        partial(spread_rows_kernel, width, [(x.shape[1], count) for x, _ in pairs]),
        name,
        [(x, (total, x.shape[1]), lambda i: (place, 0)) for x, _ in pairs]
        + [spec for _, specs in pairs for spec in specs],
        [(shape, BF, None, None)] * 2,
        (1,),
        waits=waits,
    )


def hidden_kernel(cols, steps, own, mate, *refs):
    pieces, target = refs[:-1], refs[-1]
    at = pl.program_id(0)
    half = len(pieces) // 2

    @pl.when(at < steps)
    def _():
        target[...] = dot_nn(own[...], join(pieces, slice(0, cols)))

    @pl.when(at >= steps)
    def _():
        turned = pieces[half:] + pieces[:half]
        target[...] = dot_nn(mate[...], join(turned, slice(0, cols)))


def hidden_side(own, mate, pieces, cols, waits=()):
    rows, features = own.shape
    block = min(256, rows)
    steps = rows // block
    return call(
        partial(hidden_kernel, lanes(cols), steps),
        "hidden_side",
        [
            (own, (block, features), lambda i: (jnp.minimum(i, steps - 1), 0)),
            (mate, (block, features), lambda i: (jnp.maximum(i - steps, 0), 0)),
        ]
        + right_part(pieces, cols),
        [((2 * rows, lanes(cols)), F32, (block, lanes(cols)), lambda i: (i, 0))],
        (2 * steps,),
        waits=waits,
    )[0]


def units_kernel(count, own, mate, grad, *refs):
    gates, ups = refs[:count], refs[count : 2 * count]
    hidden, gate_grad, up_grad = refs[2 * count :]
    rows = own.shape[0]
    half = count // 2
    for source, turn, place in ((own, 0, slice(0, rows)), (mate, half, slice(rows, 2 * rows))):
        value = source[...]
        a = dot_nn(value, join(gates[turn:] + gates[:turn]))
        b = dot_nn(value, join(ups[turn:] + ups[:turn]))
        inner = 0.7978845608028654 * (a + 0.044715 * (a * a * a))
        tanh = jnp.tanh(inner)
        cdf = 0.5 * (1.0 + tanh)
        gelu = a * cdf
        slope = cdf + 0.5 * a * (1.0 - tanh * tanh) * 0.7978845608028654 * (
            1.0 + 3.0 * 0.044715 * (a * a)
        )
        dh = grad[place, :]
        hidden[place, :] = (gelu * b).astype(BF)
        gate_grad[place, :] = (dh * b * slope).astype(BF)
        up_grad[place, :] = (dh * gelu).astype(BF)


def unit_rows(own, mate, gates, ups, grad, place, into=(), waits=()):
    rows, features = own.shape
    units = grad.shape[1]
    width = gates[0].shape[0]
    tile = min(256, units)
    by_tile = lambda j: (0, j)
    return call(
        partial(units_kernel, len(gates)),
        "unit_rows",
        [(own, None, None), (mate, None, None), (grad, (2 * rows, tile), by_tile)]
        + [(p, (width, tile), by_tile) for p in (*gates, *ups)],
        [((4 * rows, units), BF, (2 * rows, tile), lambda j: (place, j))] * 3,
        (pl.cdiv(units, tile),),
        waits=waits,
        into=into,
    )


def join_kernel(order, own, mate, pair, both, target):
    count = len(order)
    width = own.shape[1] // count
    rows = own.shape[0]
    for i, part in enumerate((own, mate, pair, both)):
        for at, number in enumerate(order):
            place = (number + count // 2) % count if i % 2 else number
            target[i * rows : (i + 1) * rows, at * width : (at + 1) * width] = part[
                :, place * width : (place + 1) * width
            ]


def block_order(bits):
    count = lax.axis_size("wide")
    return sorted(range(count), key=lambda j: tuple(j >> b & 1 for b in bits) + (j,))


def join_rows(parts, bits, waits=()):
    rows, features = parts[0].shape
    return call(
        partial(join_kernel, block_order(bits)),
        "join_rows",
        [(x, None, None) for x in parts],
        [((4 * rows, features), BF, None, None)],
        (1,),
        waits=waits,
    )[0]


def row_major(array):
    return with_layout_constraint(array, Layout(tuple(range(array.ndim))))


def weight_grads(left, right):
    count = lax.axis_size("wide")
    half = left.shape[1] // 2

    def part(columns):
        value = jnp.einsum("na,nb->ab", columns, right, preferred_element_type=F32).astype(BF)
        return row_major(value.reshape(count // 2, -1, right.shape[1]))

    return part(left[:, half:]), part(left[:, :half])


def branch_kernel(heads, cols, rows, z, mixed, *refs):
    pieces, dz, down = refs[:-2], refs[-2], refs[-1]
    dy = dot_nn(rows[...], join(pieces, slice(0, cols)))
    for h in range(heads):
        at = slice(h * VAL, (h + 1) * VAL)
        grouped, inverse = normalize(mixed[h])
        gate, upstream = z[:, at], dy[:, at]
        sig = jax.nn.sigmoid(gate)
        dz[:, at] = (upstream * grouped * (sig + gate * sig * (1.0 - sig))).astype(BF)
        dg = upstream * (gate * sig)
        first = jnp.mean(dg, axis=-1, keepdims=True)
        second = jnp.mean(dg * grouped, axis=-1, keepdims=True)
        down[h] = (inverse * (dg - first - grouped * second)).astype(BF)
    fill(dz, cols, dz.shape[1])


def branch_back(rows, z, mixed, pieces, waits=()):
    heads, total, _ = mixed.shape
    cols = heads * VAL
    block = min(256, total)
    by_rows = lambda i: (i, 0)
    by_heads = lambda i: (0, i, 0)
    return call(
        partial(branch_kernel, heads, cols),
        "branch_back",
        [
            (rows, (block, rows.shape[1]), by_rows),
            (z, (block, cols), by_rows),
            (mixed, (heads, block, VAL), by_heads),
        ]
        + right_part(pieces, cols),
        [
            ((total, lanes(cols)), BF, (block, lanes(cols)), by_rows),
            ((heads, total, VAL), BF, (heads, block, VAL), by_heads),
        ],
        (total // block,),
        waits=waits,
    )


def weight_block(rate, row_seg, col_seg, offset, block):
    down = lax.broadcasted_iota(jnp.int32, (block, block), 0)
    across = lax.broadcasted_iota(jnp.int32, (block, block), 1)
    gap = offset + down - across
    allowed = (gap >= 0) & (row_seg == col_seg)
    return jnp.where(allowed, jnp.exp(-rate * jnp.maximum(gap, 0).astype(F32)), 0.0)


def normalize(mixed):
    centred = mixed - jnp.mean(mixed, axis=-1, keepdims=True)
    inverse = lax.rsqrt(jnp.mean(centred * centred, axis=-1, keepdims=True) + 1.0)
    return centred * inverse, inverse


def forward_kernel(block, steps, heads, ends, rate, seg_col, seg_row, qkv, z, gated, mixed, values, acc):
    at = pl.program_id(0)
    rows = pl.ds(pl.multiple_of(at * block, block), block)
    key_at, val_at = heads * KEY, 2 * heads * KEY

    @pl.when(at == 0)
    def _():
        for h in range(heads):
            values[h] = qkv[:, val_at + h * VAL : val_at + (h + 1) * VAL]

    acc[...] = jnp.zeros_like(acc)
    for step in range(steps):

        @pl.when((step <= at) & (ends[steps + step] >= ends[at]))
        def _():
            cols = pl.ds(step * block, block)
            for h in range(heads):
                weight = weight_block(
                    rate[0:1, h : h + 1], seg_col[...], seg_row[:, cols], (at - step) * block, block
                )
                q = qkv[rows, h * KEY : (h + 1) * KEY]
                k = qkv[cols, key_at + h * KEY : key_at + (h + 1) * KEY]
                probs = (dot_nt(q, k) * weight).astype(BF)
                acc[h] += dot_nn(probs, values[h, cols, :])

    for h in range(heads):
        total = acc[h]
        grouped, _ = normalize(total)
        mixed[h] = total
        gate = z[:, h * VAL : (h + 1) * VAL]
        gated[:, h * VAL : (h + 1) * VAL] = (gate * jax.nn.sigmoid(gate) * grouped).astype(BF)
    fill(gated, heads * VAL, gated.shape[1])


def retain_forward(qkv, z, seg_row, seg_col, rate, waits=()):
    total = qkv.shape[0]
    heads = rate.shape[1]
    block = min(256, total)
    steps = total // block
    by_rows = lambda i, *t: (i, 0)
    by_heads = lambda i, *t: (0, i, 0)
    ends = jnp.concatenate([seg_row[0, ::block], seg_row[0, block - 1 :: block]])
    return call(
        partial(forward_kernel, block, steps, heads),
        "retain_forward",
        [
            (rate, None, None),
            (seg_col, (block, 1), by_rows),
            (seg_row, None, None),
            (qkv, None, None),
            (z, (block, heads * VAL), by_rows),
        ],
        [
            ((total, lanes(heads * VAL)), BF, (block, lanes(heads * VAL)), by_rows),
            ((heads, total, VAL), F32, (heads, block, VAL), by_heads),
        ],
        (steps,),
        [pltpu.VMEM((heads, total, VAL), BF), pltpu.VMEM((heads, block, VAL), F32)],
        waits,
        ends,
    )


def backward_kernel(
    block, steps, heads, ends, rate, seg_col, seg_row, qkv, down, grads, val_grads, values, dk_acc, dv_acc, dq_acc
):
    at = pl.program_id(0)
    rows = pl.ds(pl.multiple_of(at * block, block), block)
    key_at, val_at = heads * KEY, 2 * heads * KEY

    @pl.when(at == 0)
    def _():
        dk_acc[...] = jnp.zeros_like(dk_acc)
        dv_acc[...] = jnp.zeros_like(dv_acc)
        for h in range(heads):
            values[h] = qkv[:, val_at + h * VAL : val_at + (h + 1) * VAL]

    dq_acc[...] = jnp.zeros_like(dq_acc)
    for step in range(steps):

        @pl.when((step <= at) & (ends[steps + step] >= ends[at]))
        def _():
            cols = pl.ds(step * block, block)
            for h in range(heads):
                weight = weight_block(
                    rate[0:1, h : h + 1], seg_col[...], seg_row[:, cols], (at - step) * block, block
                )
                q = qkv[rows, h * KEY : (h + 1) * KEY]
                k = qkv[cols, key_at + h * KEY : key_at + (h + 1) * KEY]
                probs = (dot_nt(q, k) * weight).astype(BF)
                score_grad = (dot_nt(down[h], values[h, cols, :]) * weight).astype(BF)
                dq_acc[h] += dot_nn(score_grad, k)
                dk_acc[h, cols, :] += dot_tn(score_grad, q)
                dv_acc[h, cols, :] += dot_tn(probs, down[h])

    for h in range(heads):
        grads[rows, h * KEY : (h + 1) * KEY] = dq_acc[h].astype(BF)

    @pl.when(at == steps - 1)
    def _():
        for h in range(heads):
            grads[:, key_at + h * KEY : key_at + (h + 1) * KEY] = dk_acc[h].astype(BF)
            val_grads[:, h * VAL : (h + 1) * VAL] = dv_acc[h].astype(BF)
        fill(val_grads, heads * VAL, val_grads.shape[1])


def retain_backward(qkv, down, seg_row, seg_col, rate, waits=()):
    total = qkv.shape[0]
    heads = rate.shape[1]
    block = min(256, total)
    steps = total // block
    ends = jnp.concatenate([seg_row[0, ::block], seg_row[0, block - 1 :: block]])
    return call(
        partial(backward_kernel, block, steps, heads),
        "retain_backward",
        [
            (rate, None, None),
            (seg_col, (block, 1), lambda i, *t: (i, 0)),
            (seg_row, None, None),
            (qkv, None, None),
            (down, (heads, block, VAL), lambda i, *t: (0, i, 0)),
        ],
        [((total, 2 * heads * KEY), BF, None, None), ((total, lanes(heads * VAL)), BF, None, None)],
        (steps,),
        [
            pltpu.VMEM((heads, total, VAL), BF),
            pltpu.VMEM((heads, total, KEY), F32),
            pltpu.VMEM((heads, total, VAL), F32),
            pltpu.VMEM((heads, block, KEY), F32),
        ],
        waits,
        ends,
    )


def swap_wide(array, mask):
    count = lax.axis_size("wide")
    return lax.ppermute(array, "wide", [(i, i ^ mask) for i in range(count)])


def swap_tensor(array, mask):
    count = lax.axis_size("tensor")
    return lax.ppermute(array, "tensor", [(i, i ^ mask) for i in range(count)])


def top_bit():
    return lax.axis_size("wide").bit_length() - 2


def mask_of(bit):
    return 1 if bit == top_bit() else 2 << bit


def double(first, second, bits, cores, sync, late=()):
    top = 1 << top_bit()
    mates_first, mates_second = {}, {}
    new = (0, 0)

    def to_mates(sync):
        mates_first[new[0] | top] = swap_wide(first[new[0]], 1)
        mates_second[new[1] | top] = swap_wide(second[new[1]], 1)
        return (mates_first[new[0] | top], mates_second[new[1] | top])

    for place, (bit_first, bit_second) in enumerate(bits):
        count = len(first)
        for step, (one, two) in enumerate(zip(list(first), list(second))):
            if place == len(bits) - 1 and step == count - 1:
                sync = (*sync, *late)
            sent = after((first[one], second[two]), *sync) if sync else (first[one], second[two])
            sync = to_mates(sync) if cores else ()
            new = (one | 1 << bit_first, two | 1 << bit_second)
            first[new[0]] = swap_wide(sent[0], mask_of(bit_first))
            second[new[1]] = swap_wide(sent[1], mask_of(bit_second))
            sync = (first[new[0]], second[new[1]], *sync)
    if cores:
        sync = to_mates(sync)
        first.update(mates_first)
        second.update(mates_second)
    return sync


def listed(pieces):
    return [pieces[number] for number in range(len(pieces))]


def far_pairs():
    count = lax.axis_size("tensor")
    return [[i, i ^ 2] for i in range(count) if not i & 2]


def choose(straight, left, right):
    return jnp.where(straight, left, right), jnp.where(straight, right, left)


def exchange_units(block, got, even):
    own, given = choose(even, block, got)
    return {0: own}, {0: swap_wide(given, 1)}


def widen_units(pieces, cols, parts):
    mask = 4
    while mask < lax.axis_size("tensor"):
        pieces = {n: beside(p, swap_tensor(p, mask), cols, parts) for n, p in pieces.items()}
        cols *= 2
        mask *= 2
    return pieces


def beside(left, right, cols, parts):
    step = round_up(cols, 128)
    rest = jnp.zeros((left.shape[0], round_up(2 * cols, 128) - 2 * cols), left.dtype)
    out = []
    for i in range(parts):
        at = slice(i * step, i * step + cols)
        out += [left[:, at], right[:, at], rest]
    return jnp.concatenate(out, axis=1)


def fold(kept, got, low=False):
    half = kept.shape[0] // 2
    places = (slice(1, None, 2), slice(0, None, 2)) if low else (slice(half, None), slice(0, half))
    away, stay = (
        row_major((kept[p].astype(F32) + got[p].astype(F32)).astype(BF)) for p in places
    )
    return away, stay


def reduce_step(away, kept, bit, low=False):
    return fold(kept, swap_wide(away, mask_of(bit)), low)


def reduce_last(away, kept, bit, waits):
    got = swap_wide(away, mask_of(bit))[0]
    return kept[0].astype(F32) + after(got, *waits).astype(F32)


def reduce_chip(away, kept, bits, waits):
    for place, bit in enumerate(bits):
        got = swap_wide(away, mask_of(bit))
        if place in waits:
            got = after(got, *waits[place])
        away, kept = fold(kept, got)
    return kept[0], away[0]


def reduce_units(own, mate, cols, straight):
    mask = lax.axis_size("tensor") // 2
    while mask >= 4:
        cols //= 2
        own, mate = (
            (
                p[:, :cols].astype(F32) + swap_tensor(p[:, cols : 2 * cols], mask).astype(F32)
            ).astype(BF)
            for p in (own, mate)
        )
        mask //= 2
    return jnp.stack(choose(straight, own, swap_wide(mate, 1)))


def add_pair(pair):
    return pair[0].astype(F32) + pair[1].astype(F32)


def after(value, *earlier):
    return lax.optimization_barrier((value, earlier))[0]


def sum_all(array):
    mask = 1
    while mask < lax.axis_size("tensor"):
        array = array + swap_tensor(array, mask)
        mask *= 2
    mask = 1
    while mask < lax.axis_size("wide"):
        array = array + swap_wide(array, mask)
        mask *= 2
    return array


def body(
    tokens,
    query_weight,
    key_weight,
    value_weight,
    swish_weight,
    output_weight,
    mlp_gate,
    mlp_up,
    mlp_down,
    gain_one,
    gain_two,
    segments,
    decay_rate,
    cotangent,
):
    wide = lax.axis_size("wide")
    me = lax.axis_index("wide")
    top = top_bit()
    chip_bits = list(range(top))
    turned = chip_bits[::-1]
    numbers = jnp.arange(wide, dtype=jnp.int32)
    index = me ^ (((numbers << 1) & (wide - 1)) | (numbers >> top))
    features = tokens.shape[1]
    width = features // wide

    heads = query_weight.shape[1] // KEY
    key_cols = heads * KEY
    val_cols = heads * VAL
    own_units = mlp_gate.shape[1]
    val_pad = lanes(val_cols)
    rate = decay_rate.reshape(1, heads)

    rows, normed_local, gains = row_call(
        partial(entry_kernel, wide, width),
        "entry",
        index,
        [tokens, jnp.stack([gain_one, gain_two])],
        [like(tokens, BF), like(tokens, BF), jax.ShapeDtypeStruct((2, features), F32)],
    )
    normed = lax.all_gather(normed_local, "tensor", axis=0, tiled=True)
    total = normed.shape[0]

    block_a, block_b, block_u, block_g = pack(
        query_weight,
        key_weight,
        value_weight.T,
        swish_weight.T,
        output_weight,
        mlp_gate.T,
        mlp_up.T,
        mlp_down,
    )
    even = (me & 1) == 0
    straight = ((me ^ lax.axis_index("tensor") >> 1) & 1) == 0
    (upstream,) = row_call(
        partial(order_kernel, wide, width), "order", index, [cotangent], [like(cotangent, BF)]
    )
    crossing, opposite = list(zip(chip_bits, turned)), list(zip(turned, chip_bits))
    pieces_a, pieces_b = {0: block_a}, {0: block_b}
    double(pieces_a, pieces_b, crossing, True, (), (upstream,))
    pieces_a, pieces_b = listed(pieces_a), listed(pieces_b)

    qkv_cols = 2 * key_cols + val_cols
    gate_sent, up_sent, upstream_sent = after((block_g, block_u, upstream), normed)
    qkv, z = project(normed, pieces_a, pieces_b, qkv_cols, val_cols, (upstream,))
    gate_got, up_got = swap_tensor(gate_sent, 2), swap_tensor(up_sent, 2)
    upstream_pair = swap_tensor(upstream_sent, 1)
    gates_own, gates_mate = exchange_units(block_g, after(gate_got, qkv), even)
    units = own_units * lax.axis_size("tensor") // 4
    gates_own, gates_mate = (widen_units(p, own_units, 1) for p in (gates_own, gates_mate))
    double(gates_own, gates_mate, crossing[:1], False, ())
    seg_row = segments
    seg_col = segments.reshape(total, 1)
    gated, mixed = retain_forward(
        qkv, z, seg_row, seg_col, rate
    )
    early = (gates_own[1], gates_mate[1 << turned[0]])
    sync = double(gates_own, gates_mate, crossing[1:], False, (gated,))
    gates = listed({**gates_own, **{n | 1 << top: p for n, p in gates_mate.items()}})
    projected = spread(
        "project_out",
        [((gated,), right_part(pieces_b, val_pad))],
        (up_got, upstream_pair, *early),
    )
    moved_up = lax.psum_scatter(projected, "tensor", scatter_dimension=0, tiled=True)

    ups_own, ups_mate = exchange_units(block_u, up_got, even)
    ups_own, ups_mate = (widen_units(p, own_units, 2) for p in (ups_own, ups_mate))
    double(ups_own, ups_mate, opposite, False, ())
    ups = listed({**ups_own, **{n | 1 << top: p for n, p in ups_mate.items()}})
    upstream_mate = swap_wide(upstream, 1)
    upstream_both = swap_wide(upstream_pair, 1)
    down_rows = join_rows(
        (upstream, upstream_mate, upstream_pair, upstream_both), chip_bits, (projected,)
    )
    near_hidden = hidden_side(upstream, upstream_mate, ups, units, (down_rows,))
    middle, normed_two_local = row_call(
        middle_kernel,
        "middle",
        index,
        [rows, moved_up, gains],
        [like(rows, F32), like(rows, BF)],
        (near_hidden, *gates),
    )

    own = normed_two_local
    pair = swap_tensor(own, 1)
    mate = swap_wide(own, 1)
    near = unit_rows(own, mate, gates, ups, near_hidden, 0)
    unit_pad = lanes(units)

    def input_side(parts, place, waits=()):
        return spread_rows(
            "input_side",
            [(parts[1], left_part(gates, unit_pad)), (parts[2], left_part(ups, unit_pad))],
            place,
            waits,
        )

    def output_side(parts, place, waits=()):
        return spread_rows("output_side", [(parts[0], right_part(ups, unit_pad))], place, waits)

    far_hidden = hidden_side(upstream_pair, upstream_both, ups, units, (near[0],))
    pair = after(pair, far_hidden)
    both = swap_wide(pair, 1)
    hidden, gate_rows, up_rows = unit_rows(pair, both, gates, ups, far_hidden, 1, near)
    unit_parts = (hidden, gate_rows, up_rows)
    far_own, far_mate = input_side(unit_parts, 1)
    far_sent = (far_own.astype(F32) + swap_wide(far_mate, 1).astype(F32)).astype(BF)
    moved_far = swap_tensor(far_sent, 1)
    near_own, near_mate = input_side(unit_parts, 0, (far_sent,))
    near_got = swap_wide(near_mate, 1)
    unit_tokens = join_rows((own, mate, pair, both), turned, (near_own,))
    gate_away, gate_kept = weight_grads(unit_tokens, gate_rows)
    down_left = after(down_rows, gate_away)
    down_away, down_kept = weight_grads(down_left, hidden)
    middle_grad, branch_local, gain_two_part = row_call(
        middle_back_kernel,
        "middle_back",
        index,
        [near_own, near_got, moved_far, middle, upstream, gains],
        [like(rows, F32), like(rows, BF), jax.ShapeDtypeStruct((1, features), F32)],
        (down_away,),
    )
    branch_rows = lax.all_gather(branch_local, "tensor", axis=0, tiled=True)

    up_left = after(unit_tokens, branch_local)
    up_away, up_kept = weight_grads(up_left, up_rows)
    out_far_own, out_far_mate = output_side(unit_parts, 1, (up_away,))
    out_near_own, out_near_mate = output_side(unit_parts, 0, (out_far_own,))
    out_sent = (out_far_own.astype(F32) + swap_wide(out_far_mate, 1).astype(F32)).astype(BF)
    out_got = swap_wide(out_near_mate, 1)
    outs = {0: (out_near_own,)}
    gate_part = reduce_chip(gate_away, gate_kept, turned, outs)

    gate_far = reduce_units(*gate_part, units, straight)
    swish_rows, down = branch_back(branch_rows, z, mixed, pieces_b, (out_sent, gate_far))
    late = {**outs, top - 1: (swish_rows,)}
    down_part = reduce_chip(down_away, down_kept, chip_bits, late)
    up_part = reduce_chip(up_away, up_kept, turned, {n: (swish_rows,) for n in range(top)})

    def far(part):
        return reduce_units(*part, units, straight)

    def sum_far(array):
        return lax.psum_scatter(array, "tensor", axis_index_groups=pairs)

    pairs = far_pairs()
    gate_sum = sum_far(after(gate_far, branch_rows))
    down_up_far = jnp.concatenate([far(down_part), far(up_part)], axis=1)
    down_up_sum = sum_far(after(down_up_far, gate_sum))
    out_moved = swap_tensor(after(out_sent, branch_rows), 1)
    qk_rows, v_rows = retain_backward(qkv, down, seg_row, seg_col, rate, (down_up_far, gate_sum))

    order_a, order_b = [top] + turned, [top] + chip_bits
    qk_parts = weight_grads(normed, qk_rows)
    v_parts = weight_grads(after(normed, qk_parts[1]), v_rows)
    swish_parts = weight_grads(after(normed, v_parts[1]), swish_rows)
    out_parts = weight_grads(after(branch_rows, swish_parts[1]), gated)
    qk_parts = reduce_step(*qk_parts, top)
    v_parts = reduce_step(*v_parts, top, True)
    total_term, gain_one_part = normed_grad(
        normed,
        gains,
        [
            ((qk_rows, v_rows), left_part(pieces_a, 2 * key_cols + val_pad)),
            ((swish_rows,), left_part(pieces_b, val_pad)),
        ],
        (*out_parts, qk_parts[0], v_parts[0]),
    )
    total_term = after(total_term, down_up_sum, out_moved)
    moved_down = lax.psum_scatter(total_term, "tensor", scatter_dimension=0, tiled=True)
    swish_parts = reduce_step(*swish_parts, top, True)
    out_parts = reduce_step(*out_parts, top)
    for bit in order_b[1:-1]:
        swish_parts = reduce_step(*swish_parts, bit, True)
    for bit in order_a[1:-1]:
        out_parts = reduce_step(*out_parts, bit)
    (layer_out,) = row_call(
        partial(out_kernel, wide, width),
        "layer_out",
        index,
        [out_near_own, out_got, out_moved, middle],
        [like(rows, BF)],
        (v_parts[0],),
    )
    for bit in order_a[1:-1]:
        qk_parts = reduce_step(*qk_parts, bit)
    for bit in order_b[1:-1]:
        v_parts = reduce_step(*v_parts, bit, True)
    (gain_parts,) = call(
        partial(gains_kernel, wide, width),
        "gains",
        [(gain_one_part, None, None), (gain_two_part, None, None)],
        [((2, features), F32, None, None)],
        (1,),
        table=index,
    )
    gain_sums = sum_all(gain_parts)
    (input_grad,) = row_call(
        partial(final_kernel, wide, width),
        "final",
        index,
        [moved_down, rows, middle_grad, gains],
        [like(rows, F32)],
        (layer_out, gain_sums),
    )
    late = (input_grad,)
    swish_sum, v_sum = (reduce_last(*p, order_b[-1], late) for p in (swish_parts, v_parts))
    output_sum, qk_sum = (reduce_last(*p, order_a[-1], late) for p in (out_parts, qk_parts))
    weight_sums = (
        qk_sum[:, :key_cols],
        qk_sum[:, key_cols:],
        v_sum[:, :val_cols],
        swish_sum[:, :val_cols],
        output_sum[:, :val_cols].T,
        gate_sum[:, :own_units].astype(F32),
        down_up_sum[width:, :own_units].astype(F32),
        down_up_sum[:width, :own_units].astype(F32).T,
    )
    return (layer_out, input_grad, *weight_sums, gain_sums[0], gain_sums[1])


def solution(mesh):
    tokens_at = P(("wide", "tensor"), None)
    by_rows = P("wide", "tensor")
    by_cols = P("tensor", "wide")
    in_specs = (
        tokens_at,
        by_rows,
        by_rows,
        by_rows,
        by_rows,
        by_cols,
        by_rows,
        by_rows,
        by_cols,
        P(),
        P(),
        P("wide", None),
        P("tensor"),
        tokens_at,
    )
    out_specs = (
        tokens_at,
        tokens_at,
        by_rows,
        by_rows,
        by_rows,
        by_rows,
        by_cols,
        by_rows,
        by_rows,
        by_cols,
        P(),
        P(),
    )
    return jax.shard_map(body, mesh=mesh, in_specs=in_specs, out_specs=out_specs, check_vma=False)
```
